32 devices in a mesh: section: 2 (over x), dev: 16 (over z, y, core).
Axes of the slice: x: 2, y: 2, z: 4, core: 2. Of those that a mesh axis runs over, the one named last changes fastest.
Arguments:
- frames: bfloat16 [512, 32, 1024], P(('section', 'dev')), may hold values from -6 to 6
- window_counts: int32 [2, 16], replicated, may hold values from 1 to 20, 256 in all within a row
- learned_queries: bfloat16 [32, 1024], replicated, may hold values from -6 to 6
- frame_kv: bfloat16 [1024, 2048], replicated, may hold values from -0.1875 to 0.1875
- query_out: bfloat16 [1024, 1024], replicated, may hold values from -0.1875 to 0.1875
- query_gain: float32 [1024], replicated, may hold values from 0.25 to 1.75
- captions: bfloat16 [2, 16, 128, 2048], P('section', 'dev'), may hold values from -6 to 6
- caption_lengths: int32 [2, 16], P('section', 'dev'), may hold values from 1 to 128
- caption_gain: float32 [2048], replicated, may hold values from 0.25 to 1.75
- w_query: bfloat16 [2048, 1024], replicated, may hold values from -0.125 to 0.125
- memory_kv: bfloat16 [1024, 2048], replicated, may hold values from -0.1875 to 0.1875
- w_output: bfloat16 [1024, 2048], replicated, may hold values from -0.1875 to 0.1875
- upstream: bfloat16 [2, 16, 128, 2048], P('section', 'dev'), may hold values from -6 to 6
Outputs:
- decoded: bfloat16 [2, 16, 128, 2048], P('section', 'dev')
- caption_grad: bfloat16 [2, 16, 128, 2048], P('section', 'dev')
- memory_grad: bfloat16 [512, 32, 1024], P(('section', 'dev'))
- kv_grad: float32 [1024, 2048], P(('section', 'dev'))
The draws below stay inside these ranges and needn't reach their ends.
Inputs may be any that keep to these rules, and one draw needn't show every extreme that they name: `window_counts`: each row sums to 256; in each row some video has exactly 20.
All inputs are finite; a program needn't handle non-finite values.
Results may differ from the reference program's by a relative error of at most 0.023.
Values may be sent and summed in bfloat16 or wider, within the bound.
A program may use at most 192 MiB of HBM per device.

```python
import math
import jax
import jax.numpy as jnp
import numpy as np
from jax import lax

DMODEL = 2048
HEADS = 16
HEAD_DIM = 64
INNER = 1024
QDIM = 1024
QHEADS = 16
QUERIES = 32
FRAMES = 32
WIN_DEV = 16
MOST_WIN = 20
SLOTS = 2
CAPLEN = 128
GROUPS = 2
VIDEOS = 16
WINDOWS = 512
N_SECTION = 2
N_DEV = 16


def place_ends(array, key, least, high):
    longest = array.shape.index(max(array.shape))
    spots = []
    for shift in (0, 1):
        where = [jax.random.randint(jax.random.fold_in(key, axis), (), 0, length) for axis, length in enumerate(array.shape)]
        where[longest] = (where[longest] + shift) % array.shape[longest]
        spots.append(tuple(where))
    return array.at[spots[0]].set(least).at[spots[1]].set(high)


def block_levels(own_key, dims, split, least, high):
    def one(dim, blocks):
        draws = jax.random.uniform(jax.random.fold_in(jax.random.fold_in(own_key, 6), dim), (blocks,), jnp.float32, least / len(split), high / len(split))
        return jnp.repeat(jnp.exp(draws), dims[dim] // blocks).reshape((-1,) + (1,) * (len(dims) - dim - 1))

    loudness = one(*split[0])
    for cut in split[1:]:
        loudness = loudness * one(*cut)
    return loudness


def profile(number_of, total, bound, slope):
    portions = [(1 << 20) // math.isqrt(rank ** slope) + 1 for rank in range(2, number_of + 1)]
    spare, given = total - bound - (number_of - 1), [1] * (number_of - 1)
    while spare > 0:
        candidates = [i for i in range(number_of - 1) if given[i] < bound]
        pool, budget = sum([portions[i] for i in candidates]), spare
        for i in candidates:
            more = min(bound - given[i], max(1, budget * portions[i] // pool), spare)
            given[i] = given[i] + more
            spare = spare - more
    return np.array([bound] + given)


def ragged(rng, number_of, total, most, lean):
    if number_of == 2:
        one = jax.random.randint(rng, (), max(1, total - most), min(most, total - 1) + 1)
        return jnp.stack([one, total - one])
    sizes = jnp.asarray(profile(number_of, total, most, lean), jnp.int32)
    couples = (number_of - 1) // 2
    giver, sink = sizes[1:1 + 2 * couples:2], sizes[2:2 + 2 * couples:2]
    room = jnp.minimum(giver - 1, most - sink)
    shifted = jax.random.randint(jax.random.fold_in(rng, 1), (couples,), 0, 1 << 20) % (room + 1)
    sizes = sizes.at[1:1 + 2 * couples:2].set(giver - shifted).at[2:2 + 2 * couples:2].set(sink + shifted)
    return sizes[jax.random.permutation(jax.random.fold_in(rng, 2), number_of)]


def normal_values(stream_key, extent, spread, most, shards=(), kind=jnp.bfloat16):
    entries = spread * jax.random.normal(stream_key, extent, jnp.float32)
    if shards:
        entries = entries * block_levels(stream_key, extent, shards, -0.22, 0.18)
    return jnp.clip(entries, -most, most).astype(kind)


def setup_inputs(seed: int = 0) -> dict:
    streams_of = jax.random.split(jax.random.key(seed), 14)
    frames = normal_values(streams_of[0], (WINDOWS, FRAMES, QDIM), 1.0, 6.0, ((0, 32),))
    window_counts = jax.vmap(lambda own: ragged(own, VIDEOS, WIN_DEV * N_DEV, MOST_WIN, 2))(jax.random.split(streams_of[1], GROUPS)).reshape((GROUPS, VIDEOS)).astype(jnp.int32)
    learned_queries = normal_values(streams_of[2], (QUERIES, QDIM), 1.0, 6.0)
    frame_kv = normal_values(streams_of[3], (QDIM, 2 * QDIM), QDIM ** -0.5, 0.1875)
    query_out = normal_values(streams_of[4], (QDIM, QDIM), QDIM ** -0.5, 0.1875)
    query_gain = jnp.clip(1.0 + 0.15 * jax.random.normal(streams_of[5], (QDIM,), jnp.float32), 0.25, 1.75)
    captions = normal_values(streams_of[6], (GROUPS, VIDEOS, CAPLEN, DMODEL), 1.0, 6.0, ((0, 2), (1, 16)))
    caption_lengths = place_ends(jax.random.randint(streams_of[7], (GROUPS, VIDEOS), 1, CAPLEN + 1), jax.random.fold_in(streams_of[7], 1), 1, CAPLEN).astype(jnp.int32)
    caption_gain = jnp.clip(1.0 + 0.15 * jax.random.normal(streams_of[8], (DMODEL,), jnp.float32), 0.25, 1.75)
    w_query = normal_values(streams_of[9], (DMODEL, INNER), DMODEL ** -0.5, 0.125)
    memory_kv = normal_values(streams_of[10], (QDIM, 2 * INNER), QDIM ** -0.5, 0.1875)
    w_output = normal_values(streams_of[11], (INNER, DMODEL), INNER ** -0.5, 0.1875)
    upstream = normal_values(streams_of[12], (GROUPS, VIDEOS, CAPLEN, DMODEL), 1.0, 6.0, ((0, 2), (1, 16)))
    return {"frames": frames, "window_counts": window_counts, "learned_queries": learned_queries, "frame_kv": frame_kv, "query_out": query_out, "query_gain": query_gain, "captions": captions, "caption_lengths": caption_lengths, "caption_gain": caption_gain, "w_query": w_query, "memory_kv": memory_kv, "w_output": w_output, "upstream": upstream}


EPSILON = 1e-06

def rms_scale(values, gain):
    return values * lax.rsqrt(lax.optimization_barrier(jnp.mean(values * values, axis=-1, keepdims=True)) + EPSILON) * gain

def compress_block(frames_block, learned_queries, frame_kv, query_out, query_gain):
    blocks = frames_block.shape[0]
    flat_frames = frames_block.reshape(blocks * FRAMES, QDIM)
    key_value = jnp.dot(flat_frames, frame_kv, preferred_element_type=jnp.float32).astype(jnp.bfloat16)
    key_heads = key_value[:, :QDIM].reshape(blocks, FRAMES, QHEADS, HEAD_DIM)
    value_heads = key_value[:, QDIM:].reshape(blocks, FRAMES, QHEADS, HEAD_DIM)
    query_heads = learned_queries.reshape(QUERIES, QHEADS, HEAD_DIM)
    scores = jnp.einsum('qhe,nfhe->nhqf', query_heads.astype(jnp.float32), key_heads.astype(jnp.float32)) * HEAD_DIM ** (-0.5)
    attention = jax.nn.softmax(scores, axis=-1).astype(jnp.bfloat16)
    context = jnp.einsum('nhqf,nfhe->nqhe', attention.astype(jnp.float32), value_heads.astype(jnp.float32)).astype(jnp.bfloat16)
    projected = jnp.dot(context.reshape(blocks * QUERIES, QDIM), query_out, preferred_element_type=jnp.float32)
    hidden = learned_queries.astype(jnp.float32)[None] + projected.reshape(blocks, QUERIES, QDIM)
    return rms_scale(hidden, query_gain).astype(jnp.bfloat16)

def attend(tokens, length, upstream, key_heads, value_heads, key_live, caption_gain, w_query, w_output):
    source = tokens.astype(jnp.float32)
    inv_rms = lax.rsqrt(lax.optimization_barrier(jnp.mean(source * source, axis=-1, keepdims=True)) + EPSILON)
    normed = (source * inv_rms * caption_gain).astype(jnp.bfloat16)
    query_heads = jnp.dot(normed, w_query, preferred_element_type=jnp.float32).astype(jnp.bfloat16).reshape(CAPLEN, HEADS, HEAD_DIM)
    scores = jnp.einsum('lhe,mhe->hlm', query_heads.astype(jnp.float32), key_heads.astype(jnp.float32)) * HEAD_DIM ** (-0.5)
    scores = jnp.where(key_live[None, None, :], scores, jnp.float32(-1e+30))
    attention = jax.nn.softmax(scores, axis=-1)
    weights = attention.astype(jnp.bfloat16)
    context = jnp.einsum('hlm,mhe->lhe', weights.astype(jnp.float32), value_heads.astype(jnp.float32)).astype(jnp.bfloat16).reshape(CAPLEN, INNER)
    decoded = (source + jnp.dot(context, w_output, preferred_element_type=jnp.float32)).astype(jnp.bfloat16)
    row_live = jnp.arange(CAPLEN, dtype=jnp.int32) < length
    grad_out = jnp.where(row_live[:, None], upstream, jnp.zeros_like(upstream))
    d_context = jnp.dot(grad_out, w_output.T, preferred_element_type=jnp.float32).astype(jnp.bfloat16).reshape(CAPLEN, HEADS, HEAD_DIM)
    d_probs = jnp.einsum('lhe,mhe->hlm', d_context.astype(jnp.float32), value_heads.astype(jnp.float32))
    d_scores = (attention * (d_probs - lax.optimization_barrier(jnp.sum(d_probs * attention, axis=-1, keepdims=True))) * HEAD_DIM ** (-0.5)).astype(jnp.bfloat16)
    d_query = jnp.einsum('hlm,mhe->lhe', d_scores.astype(jnp.float32), key_heads.astype(jnp.float32)).astype(jnp.bfloat16).reshape(CAPLEN, INNER)
    d_keys = jnp.einsum('hlm,lhe->mhe', d_scores.astype(jnp.float32), query_heads.astype(jnp.float32))
    d_values = jnp.einsum('hlm,lhe->mhe', weights.astype(jnp.float32), d_context.astype(jnp.float32))
    rows_total = key_heads.shape[0]
    d_pair = jnp.concatenate([d_keys.reshape(rows_total, INNER), d_values.reshape(rows_total, INNER)], axis=1).astype(jnp.bfloat16)
    d_scaled = jnp.dot(d_query, w_query.T, preferred_element_type=jnp.float32) * caption_gain
    caption_grad = grad_out.astype(jnp.float32) + inv_rms * (d_scaled - source * inv_rms * inv_rms * lax.optimization_barrier(jnp.mean(d_scaled * source, axis=-1, keepdims=True)))
    return (decoded, caption_grad.astype(jnp.bfloat16), d_pair)

def reference(frames, window_counts, learned_queries, frame_kv, query_out, query_gain, captions, caption_lengths, caption_gain, w_query, memory_kv, w_output, upstream):
    senders = N_SECTION * N_DEV
    memory = lax.map(lambda block: compress_block(block, learned_queries, frame_kv, query_out, query_gain), frames.reshape(senders, WIN_DEV, FRAMES, QDIM)).reshape(WINDOWS, QUERIES, QDIM)
    run_ends = jnp.cumsum(window_counts, axis=1).astype(jnp.int32)
    starts = (run_ends - window_counts).astype(jnp.int32)
    position = jnp.arange(MOST_WIN, dtype=jnp.int32)
    ranked = starts[:, :, None] + position[None, None, :]
    sender = ranked // SLOTS % N_DEV
    local_index = ranked // (SLOTS * N_DEV) * SLOTS + ranked % SLOTS
    group_index = jnp.arange(GROUPS, dtype=jnp.int32)[:, None, None]
    window_id = (group_index * N_DEV + sender) * WIN_DEV + local_index
    present = position[None, None, :] < window_counts[:, :, None]
    window_id = jnp.where(present, window_id, jnp.zeros_like(window_id)).astype(jnp.int32)
    halves = jnp.take(memory, window_id.reshape(-1), axis=0).reshape(GROUPS, VIDEOS, MOST_WIN, QUERIES, QDIM)
    halves = jnp.where(present[:, :, :, None, None], halves, jnp.zeros_like(halves))
    token_pos = jnp.arange(MOST_WIN * QUERIES, dtype=jnp.int32) // QUERIES

    def per_video(carry, inputs):
        video_halves, counts, tokens, lengths, grads = inputs
        flat_halves = video_halves.reshape(GROUPS * MOST_WIN * QUERIES, QDIM)
        key_value = jnp.dot(flat_halves, memory_kv, preferred_element_type=jnp.float32).astype(jnp.bfloat16)
        key_heads = key_value[:, :INNER].reshape(-1, HEADS, HEAD_DIM)
        value_heads = key_value[:, INNER:].reshape(-1, HEADS, HEAD_DIM)
        key_live = (token_pos[None, :] < counts[:, None]).reshape(-1)
        decoded, caption_grad, d_pair = lax.map(lambda item: attend(item[0], item[1], item[2], key_heads, value_heads, key_live, caption_gain, w_query, w_output), (tokens, lengths, grads))
        d_sum = lax.optimization_barrier(jnp.sum(d_pair.astype(jnp.float32), axis=0)).astype(jnp.bfloat16)
        d_memory = jnp.dot(d_sum, memory_kv.T, preferred_element_type=jnp.float32).astype(jnp.bfloat16)
        weight_term = jnp.dot(flat_halves.T, d_sum, preferred_element_type=jnp.float32)
        return (carry + weight_term, (decoded, caption_grad, d_memory.reshape(GROUPS, MOST_WIN, QUERIES, QDIM)))
    inputs = (jnp.moveaxis(halves, 1, 0), window_counts.T, jnp.moveaxis(captions, 1, 0), caption_lengths.T, jnp.moveaxis(upstream, 1, 0))
    kv_grad, outputs = lax.scan(per_video, jnp.zeros((QDIM, 2 * INNER), jnp.float32), inputs)
    decoded = jnp.moveaxis(outputs[0], 0, 1)
    caption_grad = jnp.moveaxis(outputs[1], 0, 1)
    d_memory = jnp.moveaxis(outputs[2], 0, 1).reshape(GROUPS * VIDEOS * MOST_WIN, QUERIES, QDIM)
    window_all = jnp.arange(WINDOWS, dtype=jnp.int32)
    group_of = window_all // (N_DEV * WIN_DEV)
    device_of = window_all // WIN_DEV % N_DEV
    slot_of = window_all % WIN_DEV
    rank_of = slot_of // SLOTS * (SLOTS * N_DEV) + device_of * SLOTS + slot_of % SLOTS
    group_ends = jnp.take(run_ends, group_of, axis=0)
    owner_video = lax.optimization_barrier(jnp.sum((group_ends <= rank_of[:, None]).astype(jnp.int32), axis=1)).astype(jnp.int32)
    owner_start = jnp.take(starts.reshape(-1), group_of * VIDEOS + owner_video)
    flat_index = ((group_of * VIDEOS + owner_video) * MOST_WIN + rank_of - owner_start).astype(jnp.int32)
    memory_grad = jnp.take(d_memory, flat_index, axis=0)
    return (decoded, caption_grad, memory_grad, kv_grad)
```

```python
import jax
import jax.numpy as jnp
from jax import lax
from jax.experimental import pallas as pl
from jax.experimental.pallas import tpu as pltpu
from jax.sharding import PartitionSpec as P

HEAD_DIM = 64
MOST_WIN = 20
EPSILON = 1e-06
SCALE = HEAD_DIM ** (-0.5)
NT = (((1,), (1,)), ((), ()))
TN = (((0,), (0,)), ((), ()))
LANES = 128
VMEM = 60 * 1024 * 1024


def dot(a, b, dims=(((1,), (0,)), ((), ()))):
    return lax.dot_general(a, b, dims, preferred_element_type=jnp.float32)


def half_lanes(x, which):
    lane = lax.broadcasted_iota(jnp.int32, x.shape, 1)
    return jnp.where(lane // HEAD_DIM == which, x, jnp.zeros_like(x))


def compress_kernel(
    index_ref, frames_ref, queries_ref, kv_ref, out_w_ref, gain_ref, packed_ref, kv_s, ctx_s, mem_s
):
    step = pl.program_id(0)
    group, frames, width = frames_ref.shape
    tokens = queries_ref.shape[0]
    kv_s[...] = dot(frames_ref[...].reshape(group * frames, width), kv_ref[...]).astype(jnp.bfloat16)
    heads = 4
    span = heads * HEAD_DIM
    lane = lax.broadcasted_iota(jnp.int32, (tokens, span), 1) // HEAD_DIM
    for part in range(width // span):
        lo = part * span
        queries = queries_ref[:, lo : lo + span]
        stacked = jnp.concatenate(
            [jnp.where(lane == h, queries, jnp.zeros_like(queries)) for h in range(heads)], axis=0
        )
        scores = dot(kv_s[:, lo : lo + span], stacked, NT) * SCALE
        scores = scores.reshape(group, frames, heads * tokens)
        weights = jnp.exp(scores - jnp.max(scores, axis=1, keepdims=True))
        weights = (weights / jnp.sum(weights, axis=1, keepdims=True)).astype(jnp.bfloat16)
        for w in range(group):
            rows = slice(w * frames, (w + 1) * frames)
            every = dot(weights[w], kv_s[rows, width + lo : width + lo + span], TN)
            mixed = every[:tokens]
            for h in range(1, heads):
                mixed = jnp.where(lane == h, every[h * tokens : (h + 1) * tokens], mixed)
            ctx_s[w * tokens : (w + 1) * tokens, lo : lo + span] = mixed.astype(jnp.bfloat16)
    projected = dot(ctx_s[...], out_w_ref[...]).reshape(group, tokens, width)
    hidden = queries_ref[...].astype(jnp.float32)[None] + projected
    scale = lax.rsqrt(jnp.mean(hidden * hidden, axis=-1, keepdims=True) + EPSILON)
    mem_s[pl.ds(step * group, group)] = (hidden * scale * gain_ref[...][None]).astype(jnp.bfloat16)

    @pl.when(step == pl.num_programs(0) - 1)
    def _():
        def place(slot, carry):
            packed_ref[slot] = mem_s[index_ref[slot]]
            return carry

        lax.fori_loop(0, packed_ref.shape[0], place, 0)


def compress(index, frames, queries, frame_kv, query_out, gain):
    windows, length, width = frames.shape
    tokens = queries.shape[0]
    slots = index.shape[0]
    group = 8
    whole = lambda *shape: pl.BlockSpec(shape, lambda i, idx: (0,) * len(shape))
    return pl.pallas_call(
        compress_kernel,
        grid_spec=pltpu.PrefetchScalarGridSpec(
            num_scalar_prefetch=1,
            grid=(windows // group,),
            in_specs=[
                pl.BlockSpec((group, length, width), lambda i, idx: (i, 0, 0)),
                whole(tokens, width),
                whole(width, 2 * width),
                whole(width, width),
                whole(1, width),
            ],
            out_specs=whole(slots, tokens, width),
            scratch_shapes=[
                pltpu.VMEM((group * length, 2 * width), jnp.bfloat16),
                pltpu.VMEM((group * tokens, width), jnp.bfloat16),
                pltpu.VMEM((windows, tokens, width), jnp.bfloat16),
            ],
        ),
        out_shape=jax.ShapeDtypeStruct((slots, tokens, width), jnp.bfloat16),
        compiler_params=pltpu.CompilerParams(vmem_limit_bytes=48 * 1024 * 1024),
        cost_estimate=pl.CostEstimate(
            flops=2 * windows * length * width * width * 4,
            bytes_accessed=12 * 1024 * 1024,
            transcendentals=0,
        ),
        name="compress",
    )(index, frames, queries, frame_kv, query_out, gain.reshape(1, width))


def gather_kernel(index_ref, live_ref, table_ref, out_ref):
    def place(row, carry):
        value = table_ref[index_ref[row]]
        out_ref[row] = jnp.where(live_ref[row] > 0, value, jnp.zeros_like(value))
        return carry

    lax.fori_loop(0, out_ref.shape[0], place, 0)


def gather(index, live, table):
    rows = index.shape[0]
    shape = (rows,) + table.shape[1:]
    return pl.pallas_call(
        gather_kernel,
        grid_spec=pltpu.PrefetchScalarGridSpec(
            num_scalar_prefetch=2,
            grid=(1,),
            in_specs=[pl.BlockSpec(table.shape, lambda i, a, b: (0, 0, 0))],
            out_specs=pl.BlockSpec(shape, lambda i, a, b: (0, 0, 0)),
        ),
        out_shape=jax.ShapeDtypeStruct(shape, table.dtype),
        compiler_params=pltpu.CompilerParams(vmem_limit_bytes=24 * 1024 * 1024),
        name="gather",
    )(index, live, table)


def masked_scores(keys, queries, live):
    scores = dot(keys, queries, NT) * SCALE
    token = lax.broadcasted_iota(jnp.int32, scores.shape, 0)
    return jnp.where(token < live, scores, jnp.float32(-1e30))


def stats_kernel(live_ref, q_ref, g_ref, k_ref, v_ref, stats_ref):
    live = live_ref[0]
    rows = []
    for h in range(2):
        scores = masked_scores(k_ref[...], half_lanes(q_ref[...], h), live)
        most = jnp.max(scores, axis=0, keepdims=True)
        weights = jnp.exp(scores - most)
        d_probs = dot(v_ref[...], half_lanes(g_ref[...], h), NT)
        rows += [
            most,
            jnp.sum(weights, axis=0, keepdims=True),
            jnp.sum(weights * d_probs, axis=0, keepdims=True),
        ]
    rows += [jnp.zeros_like(rows[0])] * 2
    stats_ref[0] = jnp.concatenate(rows, axis=0)


def grads_kernel(
    live_ref, q_ref, g_ref, k_ref, v_ref, mine_ref, peer_ref, part_ref, d_kv_ref
):
    live = live_ref[0]
    mine, peer = mine_ref[0], peer_ref[0]
    keys, values = k_ref[...], v_ref[...]
    keys_t, values_t = keys.T, values.T
    d_keys = d_values = None
    d_query, context = [], []
    for h in range(2):
        queries, d_context = half_lanes(q_ref[...], h), half_lanes(g_ref[...], h)
        at = 3 * h
        most = jnp.maximum(mine[at : at + 1], peer[at : at + 1])
        scale_mine = jnp.exp(mine[at : at + 1] - most)
        scale_peer = jnp.exp(peer[at : at + 1] - most)
        inverse = 1.0 / (
            mine[at + 1 : at + 2] * scale_mine + peer[at + 1 : at + 2] * scale_peer
        )
        dots = (
            mine[at + 2 : at + 3] * scale_mine + peer[at + 2 : at + 3] * scale_peer
        ) * inverse
        probs = jnp.exp(masked_scores(keys, queries, live) - most) * inverse
        weights = probs.astype(jnp.bfloat16)
        d_probs = dot(values, d_context, NT)
        d_scores = (probs * (d_probs - dots) * SCALE).astype(jnp.bfloat16)
        cut = slice(h * HEAD_DIM, (h + 1) * HEAD_DIM)
        context.append(dot(values_t[cut], weights))
        d_query.append(dot(keys_t[cut], d_scores))
        dk, dv = dot(d_scores, queries), dot(weights, d_context)
        d_keys = dk if d_keys is None else d_keys + dk
        d_values = dv if d_values is None else d_values + dv
    part_ref[0] = jnp.concatenate(context, axis=0).T.astype(jnp.bfloat16)
    part_ref[1] = jnp.concatenate(d_query, axis=0).T.astype(jnp.bfloat16)
    d_kv_ref[0] = d_keys.astype(jnp.bfloat16)
    d_kv_ref[1] = d_values.astype(jnp.bfloat16)


def attention_specs(rows, keys, pairs):
    column = lambda n, shift: pl.BlockSpec((n, LANES), lambda i, live: (0, i + shift))
    return [column(rows, 0), column(rows, 0), column(keys, 0), column(keys, pairs)]


def attention_stats(live, q, g, kv):
    rows, width = q.shape
    pairs = width // LANES
    return pl.pallas_call(
        stats_kernel,
        grid_spec=pltpu.PrefetchScalarGridSpec(
            num_scalar_prefetch=1,
            grid=(pairs,),
            in_specs=attention_specs(rows, kv.shape[0], pairs),
            out_specs=pl.BlockSpec((1, 8, rows), lambda i, live: (i, 0, 0)),
        ),
        out_shape=jax.ShapeDtypeStruct((pairs, 8, rows), jnp.float32),
        compiler_params=pltpu.CompilerParams(vmem_limit_bytes=32 * 1024 * 1024),
        name="attention_stats",
    )(live, q, g, kv, kv)


def attention_grads(live, q, g, kv, mine, peer):
    rows, width = q.shape
    keys = kv.shape[0]
    pairs = width // LANES
    stats = pl.BlockSpec((1, 8, rows), lambda i, live: (i, 0, 0))
    return pl.pallas_call(
        grads_kernel,
        grid_spec=pltpu.PrefetchScalarGridSpec(
            num_scalar_prefetch=1,
            grid=(pairs,),
            in_specs=attention_specs(rows, keys, pairs) + [stats, stats],
            out_specs=[
                pl.BlockSpec((2, rows, LANES), lambda i, live: (0, 0, i)),
                pl.BlockSpec((2, keys, LANES), lambda i, live: (0, 0, i)),
            ],
        ),
        out_shape=[
            jax.ShapeDtypeStruct((2, rows, width), jnp.bfloat16),
            jax.ShapeDtypeStruct((2, keys, width), jnp.bfloat16),
        ],
        compiler_params=pltpu.CompilerParams(vmem_limit_bytes=32 * 1024 * 1024),
        name="attention_grads",
    )(live, q, g, kv, kv, mine, peer)


def swap(x):
    return lax.ppermute(x, "section", [(0, 1), (1, 0)])


def local(
    frames,
    window_counts,
    learned_queries,
    frame_kv,
    query_out,
    query_gain,
    captions,
    caption_lengths,
    caption_gain,
    w_query,
    memory_kv,
    w_output,
    upstream,
):
    videos = lax.axis_size("dev")
    windows, _, width = frames.shape
    tokens = learned_queries.shape[0]
    inner = w_query.shape[1]
    caplen = captions.shape[2]
    per_slot = (MOST_WIN + videos - 2) // (videos - 1)
    section_id = lax.axis_index("section")
    video_id = lax.axis_index("dev")
    counts_row = lax.dynamic_index_in_dim(window_counts, section_id, 0, keepdims=False)
    run_ends = jnp.cumsum(counts_row)
    starts = run_ends - counts_row
    local_index = jnp.arange(windows, dtype=jnp.int32)
    ranked = (
        local_index // per_slot * (per_slot * videos) + video_id * per_slot + local_index % per_slot
    )
    owner_video = jnp.sum((run_ends[None, :] <= ranked[:, None]).astype(jnp.int32), axis=1)
    target = owner_video * per_slot + local_index % per_slot
    slot_index = jnp.arange(videos * per_slot, dtype=jnp.int32)
    send_index = jnp.sum(
        jnp.where(slot_index[:, None] == target[None, :], local_index[None, :], 0), axis=1
    )
    count_here = lax.dynamic_index_in_dim(counts_row, video_id, 0, keepdims=False)
    start_here = lax.dynamic_index_in_dim(starts, video_id, 0, keepdims=False)
    position = jnp.arange(MOST_WIN, dtype=jnp.int32)
    incoming = start_here + position
    source_slot = incoming // per_slot % videos * per_slot + incoming % per_slot
    present = position < count_here
    return_index = jnp.sum(
        jnp.where(
            (slot_index[:, None] == source_slot[None, :]) & present[None, :], position[None, :], 0
        ),
        axis=1,
    )
    live = (count_here * tokens).reshape(1)

    x = captions[0, 0].astype(jnp.float32)
    inv_rms = lax.rsqrt(jnp.mean(x * x, axis=-1, keepdims=True) + EPSILON)
    normed = (x * inv_rms * caption_gain).astype(jnp.bfloat16)
    query = dot(normed, w_query).astype(jnp.bfloat16)
    row_live = jnp.arange(caplen, dtype=jnp.int32) < caption_lengths[0, 0]
    grad_out = jnp.where(row_live[:, None], upstream[0, 0], jnp.zeros_like(upstream[0, 0]))
    d_context = dot(grad_out, w_output, NT).astype(jnp.bfloat16)
    own = jnp.stack([query, d_context])
    both = jnp.concatenate([own, swap(own)], axis=1)

    packed = compress(send_index, frames, learned_queries, frame_kv, query_out, query_gain)
    arrived = lax.all_to_all(
        packed.reshape(videos, per_slot, tokens, width), "dev", split_axis=0, concat_axis=0, tiled=True
    ).reshape(videos * per_slot, tokens, width)
    memory_half = gather(source_slot, present.astype(jnp.int32), arrived).reshape(
        MOST_WIN * tokens, width
    )
    key_value = dot(memory_half, memory_kv).astype(jnp.bfloat16)

    stats = attention_stats(live, both[0], both[1], key_value)
    peer = swap(stats)
    peer = jnp.concatenate([peer[..., caplen:], peer[..., :caplen]], axis=-1)
    partial, d_kv = attention_grads(live, both[0], both[1], key_value, stats, peer)

    d_memory = (
        dot(d_kv[0], memory_kv[:, :inner], NT) + dot(d_kv[1], memory_kv[:, inner:], NT)
    ).astype(jnp.bfloat16)
    ones = jnp.ones_like(slot_index)
    grad_slots = gather(return_index, ones, d_memory.reshape(MOST_WIN, tokens, width))
    returned = lax.all_to_all(
        grad_slots.reshape(videos, per_slot, tokens, width),
        "dev",
        split_axis=0,
        concat_axis=0,
        tiled=True,
    ).reshape(videos * per_slot, tokens, width)
    memory_grad = gather(target, jnp.ones_like(target), returned)

    kv_terms = jnp.concatenate(
        [dot(memory_half, d_kv[0], TN), dot(memory_half, d_kv[1], TN)], axis=1
    ).astype(jnp.bfloat16)
    kv_grad = lax.psum_scatter(
        kv_terms, ("section", "dev"), scatter_dimension=0, tiled=True
    ).astype(jnp.float32)

    other = swap(partial[:, caplen:])
    merged = (
        partial[:, :caplen].astype(jnp.float32) + other.astype(jnp.float32)
    ).astype(jnp.bfloat16)
    decoded = (x + dot(merged[0], w_output)).astype(jnp.bfloat16)
    d_scaled = dot(merged[1], w_query, NT) * caption_gain
    caption_grad = grad_out.astype(jnp.float32) + inv_rms * (
        d_scaled - x * inv_rms * inv_rms * jnp.mean(d_scaled * x, axis=-1, keepdims=True)
    )
    return (
        decoded[None, None],
        caption_grad.astype(jnp.bfloat16)[None, None],
        memory_grad,
        kv_grad,
    )


def solution(mesh):
    return jax.shard_map(
        local,
        mesh=mesh,
        in_specs=(
            P(("section", "dev"), None, None),
            P(),
            P(),
            P(),
            P(),
            P(),
            P("section", "dev", None, None),
            P("section", "dev"),
            P(),
            P(),
            P(),
            P(),
            P("section", "dev", None, None),
        ),
        out_specs=(
            P("section", "dev", None, None),
            P("section", "dev", None, None),
            P(("section", "dev"), None, None),
            P(("section", "dev"), None),
        ),
        check_vma=False,
    )
```

```python
import functools

import jax
import jax.numpy as jnp
from jax import lax
from jax.experimental import pallas as pl
from jax.experimental.pallas import tpu as pltpu
from jax.sharding import PartitionSpec as P

HEAD_DIM = 64
MOST_WIN = 20
EPSILON = 1e-06
SCALE = HEAD_DIM ** (-0.5)
NT = (((1,), (1,)), ((), ()))
TN = (((0,), (0,)), ((), ()))
LANES = 128


def dot(a, b, dims=(((1,), (0,)), ((), ()))):
    return lax.dot_general(a, b, dims, preferred_element_type=jnp.float32)


def half_lanes(x, which):
    lane = lax.broadcasted_iota(jnp.int32, x.shape, 1)
    return jnp.where(lane // HEAD_DIM == which, x, jnp.zeros_like(x))


def compress_kernel(
    index_ref, frames_ref, queries_ref, kv_ref, out_w_ref, gain_ref, packed_ref, kv_s, ctx_s, mem_s
):
    step = pl.program_id(0)
    group, frames, width = frames_ref.shape
    tokens = queries_ref.shape[0]
    kv_s[...] = dot(frames_ref[...].reshape(group * frames, width), kv_ref[...]).astype(jnp.bfloat16)
    heads = 4
    span = heads * HEAD_DIM
    lane = lax.broadcasted_iota(jnp.int32, (tokens, span), 1) // HEAD_DIM
    for part in range(width // span):
        lo = part * span
        queries = queries_ref[:, lo : lo + span]
        stacked = jnp.concatenate(
            [jnp.where(lane == h, queries, jnp.zeros_like(queries)) for h in range(heads)], axis=0
        )
        scores = dot(kv_s[:, lo : lo + span], stacked, NT) * SCALE
        scores = scores.reshape(group, frames, heads * tokens)
        weights = jnp.exp(scores - jnp.max(scores, axis=1, keepdims=True))
        weights = (weights / jnp.sum(weights, axis=1, keepdims=True)).astype(jnp.bfloat16)
        for w in range(group):
            rows = slice(w * frames, (w + 1) * frames)
            every = dot(weights[w], kv_s[rows, width + lo : width + lo + span], TN)
            mixed = every[:tokens]
            for h in range(1, heads):
                mixed = jnp.where(lane == h, every[h * tokens : (h + 1) * tokens], mixed)
            ctx_s[w * tokens : (w + 1) * tokens, lo : lo + span] = mixed.astype(jnp.bfloat16)
    projected = dot(ctx_s[...], out_w_ref[...]).reshape(group, tokens, width)
    hidden = queries_ref[...].astype(jnp.float32)[None] + projected
    scale = lax.rsqrt(jnp.mean(hidden * hidden, axis=-1, keepdims=True) + EPSILON)
    mem_s[pl.ds(step * group, group)] = (hidden * scale * gain_ref[...][None]).astype(jnp.bfloat16)

    @pl.when(step == pl.num_programs(0) - 1)
    def _():
        def place(slot, carry):
            packed_ref[slot] = mem_s[index_ref[slot]]
            return carry

        lax.fori_loop(0, packed_ref.shape[0], place, 0)


def compress(index, frames, queries, frame_kv, query_out, gain):
    windows, length, width = frames.shape
    tokens = queries.shape[0]
    slots = index.shape[0]
    group = 8
    whole = lambda *shape: pl.BlockSpec(shape, lambda i, idx: (0,) * len(shape))
    return pl.pallas_call(
        compress_kernel,
        grid_spec=pltpu.PrefetchScalarGridSpec(
            num_scalar_prefetch=1,
            grid=(windows // group,),
            in_specs=[
                pl.BlockSpec((group, length, width), lambda i, idx: (i, 0, 0)),
                whole(tokens, width),
                whole(width, 2 * width),
                whole(width, width),
                whole(1, width),
            ],
            out_specs=whole(slots, tokens, width),
            scratch_shapes=[
                pltpu.VMEM((group * length, 2 * width), jnp.bfloat16),
                pltpu.VMEM((group * tokens, width), jnp.bfloat16),
                pltpu.VMEM((windows, tokens, width), jnp.bfloat16),
            ],
        ),
        out_shape=jax.ShapeDtypeStruct((slots, tokens, width), jnp.bfloat16),
        compiler_params=pltpu.CompilerParams(vmem_limit_bytes=48 * 1024 * 1024),
        cost_estimate=pl.CostEstimate(
            flops=2 * windows * length * width * width * 4,
            bytes_accessed=12 * 1024 * 1024,
            transcendentals=0,
        ),
        name="compress",
    )(index, frames, queries, frame_kv, query_out, gain.reshape(1, width))


def gather_kernel(index_ref, live_ref, table_ref, out_ref):
    def place(row, carry):
        value = table_ref[index_ref[row]]
        out_ref[row] = jnp.where(live_ref[row] > 0, value, jnp.zeros_like(value))
        return carry

    lax.fori_loop(0, out_ref.shape[0], place, 0)


def gather(index, live, table):
    rows = index.shape[0]
    shape = (rows,) + table.shape[1:]
    return pl.pallas_call(
        gather_kernel,
        grid_spec=pltpu.PrefetchScalarGridSpec(
            num_scalar_prefetch=2,
            grid=(1,),
            in_specs=[pl.BlockSpec(table.shape, lambda i, a, b: (0, 0, 0))],
            out_specs=pl.BlockSpec(shape, lambda i, a, b: (0, 0, 0)),
        ),
        out_shape=jax.ShapeDtypeStruct(shape, table.dtype),
        compiler_params=pltpu.CompilerParams(vmem_limit_bytes=24 * 1024 * 1024),
        name="gather",
    )(index, live, table)


def masked_scores(keys, queries, live):
    scores = dot(keys, queries, NT) * SCALE
    token = lax.broadcasted_iota(jnp.int32, scores.shape, 0)
    return jnp.where(token < live, scores, jnp.float32(-1e30))


def stats_kernel(live_ref, q_ref, g_ref, k_ref, v_ref, stats_ref):
    live = live_ref[0]
    rows = []
    for h in range(2):
        scores = masked_scores(k_ref[...], half_lanes(q_ref[...], h), live)
        most = jnp.max(scores, axis=0, keepdims=True)
        weights = jnp.exp(scores - most)
        d_probs = dot(v_ref[...], half_lanes(g_ref[...], h), NT)
        rows += [
            most,
            jnp.sum(weights, axis=0, keepdims=True),
            jnp.sum(weights * d_probs, axis=0, keepdims=True),
        ]
    rows += [jnp.zeros_like(rows[0])] * 2
    stats_ref[0] = jnp.concatenate(rows, axis=0)


def grads_kernel(
    live_ref, q_ref, g_ref, k_ref, v_ref, mine_ref, peer_ref, part_ref, d_kv_ref
):
    live = live_ref[0]
    mine, peer = mine_ref[0], peer_ref[0]
    keys, values = k_ref[...], v_ref[...]
    keys_t, values_t = keys.T, values.T
    d_keys = d_values = None
    d_query, context = [], []
    for h in range(2):
        queries, d_context = half_lanes(q_ref[...], h), half_lanes(g_ref[...], h)
        at = 3 * h
        most = jnp.maximum(mine[at : at + 1], peer[at : at + 1])
        scale_mine = jnp.exp(mine[at : at + 1] - most)
        scale_peer = jnp.exp(peer[at : at + 1] - most)
        inverse = 1.0 / (
            mine[at + 1 : at + 2] * scale_mine + peer[at + 1 : at + 2] * scale_peer
        )
        dots = (
            mine[at + 2 : at + 3] * scale_mine + peer[at + 2 : at + 3] * scale_peer
        ) * inverse
        probs = jnp.exp(masked_scores(keys, queries, live) - most) * inverse
        weights = probs.astype(jnp.bfloat16)
        d_probs = dot(values, d_context, NT)
        d_scores = (probs * (d_probs - dots) * SCALE).astype(jnp.bfloat16)
        cut = slice(h * HEAD_DIM, (h + 1) * HEAD_DIM)
        context.append(dot(values_t[cut], weights))
        d_query.append(dot(keys_t[cut], d_scores))
        dk, dv = dot(d_scores, queries), dot(weights, d_context)
        d_keys = dk if d_keys is None else d_keys + dk
        d_values = dv if d_values is None else d_values + dv
    part_ref[0] = jnp.concatenate(context, axis=0).T.astype(jnp.bfloat16)
    part_ref[1] = jnp.concatenate(d_query, axis=0).T.astype(jnp.bfloat16)
    d_kv_ref[0] = d_keys.astype(jnp.bfloat16)
    d_kv_ref[1] = d_values.astype(jnp.bfloat16)


def attention_specs(rows, keys, pairs):
    column = lambda n, shift: pl.BlockSpec((n, LANES), lambda i, live: (0, i + shift))
    return [column(rows, 0), column(rows, 0), column(keys, 0), column(keys, pairs)]


def attention_stats(live, q, g, kv):
    rows, width = q.shape
    pairs = width // LANES
    return pl.pallas_call(
        stats_kernel,
        grid_spec=pltpu.PrefetchScalarGridSpec(
            num_scalar_prefetch=1,
            grid=(pairs,),
            in_specs=attention_specs(rows, kv.shape[0], pairs),
            out_specs=pl.BlockSpec((1, 8, rows), lambda i, live: (i, 0, 0)),
        ),
        out_shape=jax.ShapeDtypeStruct((pairs, 8, rows), jnp.float32),
        compiler_params=pltpu.CompilerParams(vmem_limit_bytes=32 * 1024 * 1024),
        name="attention_stats",
    )(live, q, g, kv, kv)


def attention_grads(live, q, g, kv, mine, peer):
    rows, width = q.shape
    keys = kv.shape[0]
    pairs = width // LANES
    stats = pl.BlockSpec((1, 8, rows), lambda i, live: (i, 0, 0))
    return pl.pallas_call(
        grads_kernel,
        grid_spec=pltpu.PrefetchScalarGridSpec(
            num_scalar_prefetch=1,
            grid=(pairs,),
            in_specs=attention_specs(rows, keys, pairs) + [stats, stats],
            out_specs=[
                pl.BlockSpec((2, rows, LANES), lambda i, live: (0, 0, i)),
                pl.BlockSpec((2, keys, LANES), lambda i, live: (0, 0, i)),
            ],
        ),
        out_shape=[
            jax.ShapeDtypeStruct((2, rows, width), jnp.bfloat16),
            jax.ShapeDtypeStruct((2, keys, width), jnp.bfloat16),
        ],
        compiler_params=pltpu.CompilerParams(vmem_limit_bytes=32 * 1024 * 1024),
        name="attention_grads",
    )(live, q, g, kv, kv, mine, peer)


def halving_orders(bits):
    middle = list(range(bits - 1, 0, -1))
    return [bits, 0] + middle, [bits] + middle[:1] + [0] + middle[1:]


def reduce_kernel(bits, a_ref, b_ref, out_ref, *scratch):
    stages = bits + 1
    got, held = scratch[: 2 * stages], scratch[2 * stages : 4 * stages - 2]
    send_sem, recv_sem = scratch[-2:]
    section, dev = lax.axis_index("section"), lax.axis_index("dev")
    mine = [section] + [lax.rem(dev // 2 ** (bits - t), 2) for t in range(1, bits + 1)]
    peers = [(1 - section, dev)] + [
        (section, dev + (1 - 2 * mine[t]) * 2 ** (bits - t)) for t in range(1, bits + 1)
    ]
    barrier = pltpu.get_barrier_semaphore()
    for peer in peers:
        pl.semaphore_signal(barrier, inc=1, device_id=peer, device_id_type=pl.DeviceIdType.MESH)
    pl.semaphore_wait(barrier, stages)

    orders = halving_orders(bits)
    width = a_ref.shape[-1]

    def source(chain, stage):
        return (a_ref, b_ref)[chain] if stage == 0 else held[chain * (stages - 1) + stage - 1]

    def place(chain, stage):
        done = orders[chain][:stage]
        return sum(1 for t in range(orders[chain][stage]) if t not in done)

    def copy(chain, stage):
        at = (slice(None),) * place(chain, stage)
        t = orders[chain][stage]
        return pltpu.make_async_remote_copy(
            src_ref=source(chain, stage).at[at + (1 - mine[t],)],
            dst_ref=got[chain * stages + stage],
            send_sem=send_sem.at[chain * stages + stage],
            recv_sem=recv_sem.at[chain * stages + stage],
            device_id=peers[t],
            device_id_type=pl.DeviceIdType.MESH,
        )

    copies = {(c, 0): copy(c, 0) for c in range(2)}
    for c in range(2):
        copies[c, 0].start()
    for stage in range(stages):
        for c in range(2):
            copies[c, stage].wait_recv()
            left = stages - 1 - stage
            at, bit = place(c, stage), mine[orders[c][stage]]
            src, other = source(c, stage), got[c * stages + stage]

            def add(i, carry):
                index = tuple(lax.rem(i // 2 ** (left - 1 - n), 2) for n in range(left))
                total = src[index[:at] + (bit,) + index[at:]].astype(jnp.float32)
                total = total + other[index].astype(jnp.float32)
                if left:
                    held[c * (stages - 1) + stage][index] = total.astype(jnp.bfloat16)
                else:
                    out_ref[:, c * width : (c + 1) * width] = total
                return carry

            if left:
                lax.fori_loop(0, 2**left, add, 0)
                copies[c, stage + 1] = copy(c, stage + 1)
                copies[c, stage + 1].start()
            else:
                add(0, 0)
    for made in copies.values():
        made.wait_send()


def reduce_rows(a, b):
    n_section, n_dev = lax.axis_size("section"), lax.axis_size("dev")
    bits = n_dev.bit_length() - 1
    rows = a.shape[0] // (n_section * n_dev)
    width = a.shape[1]
    stages = bits + 1
    block = lambda n: pltpu.VMEM((2,) * n + (rows, width), jnp.bfloat16)
    return pl.pallas_call(
        functools.partial(reduce_kernel, bits),
        out_shape=jax.ShapeDtypeStruct((rows, 2 * width), jnp.float32),
        in_specs=[pl.BlockSpec(memory_space=pltpu.VMEM)] * 2,
        out_specs=pl.BlockSpec(memory_space=pltpu.VMEM),
        scratch_shapes=[block(stages - 1 - s) for _ in range(2) for s in range(stages)]
        + [block(stages - 1 - s) for _ in range(2) for s in range(stages - 1)]
        + [pltpu.SemaphoreType.DMA((2 * stages,)), pltpu.SemaphoreType.DMA((2 * stages,))],
        compiler_params=pltpu.CompilerParams(
            collective_id=0, has_side_effects=True, vmem_limit_bytes=32 * 1024 * 1024
        ),
        cost_estimate=pl.CostEstimate(
            flops=0, bytes_accessed=64 * 1024 * 1024, transcendentals=0
        ),
        name="reduce_rows",
    )(*(v.reshape((2,) * stages + (rows, width)) for v in (a, b)))


def swap(x):
    return lax.ppermute(x, "section", [(0, 1), (1, 0)])


def local(
    frames,
    window_counts,
    learned_queries,
    frame_kv,
    query_out,
    query_gain,
    captions,
    caption_lengths,
    caption_gain,
    w_query,
    memory_kv,
    w_output,
    upstream,
):
    videos = lax.axis_size("dev")
    windows, _, width = frames.shape
    tokens = learned_queries.shape[0]
    inner = w_query.shape[1]
    caplen = captions.shape[2]
    per_slot = (MOST_WIN + videos - 2) // (videos - 1)
    section_id = lax.axis_index("section")
    video_id = lax.axis_index("dev")
    counts_row = lax.dynamic_index_in_dim(window_counts, section_id, 0, keepdims=False)
    run_ends = jnp.cumsum(counts_row)
    starts = run_ends - counts_row
    local_index = jnp.arange(windows, dtype=jnp.int32)
    ranked = (
        local_index // per_slot * (per_slot * videos) + video_id * per_slot + local_index % per_slot
    )
    owner_video = jnp.sum((run_ends[None, :] <= ranked[:, None]).astype(jnp.int32), axis=1)
    target = owner_video * per_slot + local_index % per_slot
    slot_index = jnp.arange(videos * per_slot, dtype=jnp.int32)
    send_index = jnp.sum(
        jnp.where(slot_index[:, None] == target[None, :], local_index[None, :], 0), axis=1
    )
    count_here = lax.dynamic_index_in_dim(counts_row, video_id, 0, keepdims=False)
    start_here = lax.dynamic_index_in_dim(starts, video_id, 0, keepdims=False)
    position = jnp.arange(MOST_WIN, dtype=jnp.int32)
    incoming = start_here + position
    source_slot = incoming // per_slot % videos * per_slot + incoming % per_slot
    present = position < count_here
    return_index = jnp.sum(
        jnp.where(
            (slot_index[:, None] == source_slot[None, :]) & present[None, :], position[None, :], 0
        ),
        axis=1,
    )
    live = (count_here * tokens).reshape(1)

    x = captions[0, 0].astype(jnp.float32)
    inv_rms = lax.rsqrt(jnp.mean(x * x, axis=-1, keepdims=True) + EPSILON)
    normed = (x * inv_rms * caption_gain).astype(jnp.bfloat16)
    query = dot(normed, w_query).astype(jnp.bfloat16)
    row_live = jnp.arange(caplen, dtype=jnp.int32) < caption_lengths[0, 0]
    grad_out = jnp.where(row_live[:, None], upstream[0, 0], jnp.zeros_like(upstream[0, 0]))
    d_context = dot(grad_out, w_output, NT).astype(jnp.bfloat16)
    own = jnp.stack([query, d_context])
    both = jnp.concatenate([own, swap(own)], axis=1)

    packed = compress(send_index, frames, learned_queries, frame_kv, query_out, query_gain)
    arrived = lax.all_to_all(
        packed.reshape(videos, per_slot, tokens, width), "dev", split_axis=0, concat_axis=0, tiled=True
    ).reshape(videos * per_slot, tokens, width)
    memory_half = gather(source_slot, present.astype(jnp.int32), arrived).reshape(
        MOST_WIN * tokens, width
    )
    key_value = dot(memory_half, memory_kv).astype(jnp.bfloat16)

    stats = attention_stats(live, both[0], both[1], key_value)
    peer = swap(stats)
    peer = jnp.concatenate([peer[..., caplen:], peer[..., :caplen]], axis=-1)
    partial, d_kv = attention_grads(live, both[0], both[1], key_value, stats, peer)

    d_memory = (
        dot(d_kv[0], memory_kv[:, :inner], NT) + dot(d_kv[1], memory_kv[:, inner:], NT)
    ).astype(jnp.bfloat16)
    ones = jnp.ones_like(slot_index)
    grad_slots = gather(return_index, ones, d_memory.reshape(MOST_WIN, tokens, width))
    returned = lax.all_to_all(
        grad_slots.reshape(videos, per_slot, tokens, width),
        "dev",
        split_axis=0,
        concat_axis=0,
        tiled=True,
    ).reshape(videos * per_slot, tokens, width)
    memory_grad = gather(target, jnp.ones_like(target), returned)

    terms = [dot(memory_half, d_kv[n], TN).astype(jnp.bfloat16) for n in range(2)]
    *terms, _ = lax.optimization_barrier((*terms, grad_slots))
    kv_grad = reduce_rows(*terms)

    other = swap(partial[:, caplen:])
    merged = (
        partial[:, :caplen].astype(jnp.float32) + other.astype(jnp.float32)
    ).astype(jnp.bfloat16)
    decoded = (x + dot(merged[0], w_output)).astype(jnp.bfloat16)
    d_scaled = dot(merged[1], w_query, NT) * caption_gain
    caption_grad = grad_out.astype(jnp.float32) + inv_rms * (
        d_scaled - x * inv_rms * inv_rms * jnp.mean(d_scaled * x, axis=-1, keepdims=True)
    )
    return (
        decoded[None, None],
        caption_grad.astype(jnp.bfloat16)[None, None],
        memory_grad,
        kv_grad,
    )


def solution(mesh):
    return jax.shard_map(
        local,
        mesh=mesh,
        in_specs=(
            P(("section", "dev"), None, None),
            P(),
            P(),
            P(),
            P(),
            P(),
            P("section", "dev", None, None),
            P("section", "dev"),
            P(),
            P(),
            P(),
            P(),
            P("section", "dev", None, None),
        ),
        out_specs=(
            P("section", "dev", None, None),
            P("section", "dev", None, None),
            P(("section", "dev"), None, None),
            P(("section", "dev"), None),
        ),
        check_vma=False,
    )
```

```python
import functools

import jax
import jax.numpy as jnp
from jax import lax
from jax.experimental import pallas as pl
from jax.experimental.pallas import tpu as pltpu
from jax.sharding import PartitionSpec as P

HEAD_DIM = 64
MOST_WIN = 20
EPSILON = 1e-06
SCALE = HEAD_DIM ** (-0.5)
NT = (((1,), (1,)), ((), ()))
TN = (((0,), (0,)), ((), ()))
LANES = 128


def dot(a, b, dims=(((1,), (0,)), ((), ()))):
    return lax.dot_general(a, b, dims, preferred_element_type=jnp.float32)


def half_lanes(x, which):
    lane = lax.broadcasted_iota(jnp.int32, x.shape, 1)
    return jnp.where(lane // HEAD_DIM == which, x, jnp.zeros_like(x))


def compress_kernel(
    index_ref, frames_ref, queries_ref, kv_ref, out_w_ref, gain_ref, packed_ref, kv_s, ctx_s, mem_s
):
    step = pl.program_id(0)
    group, frames, width = frames_ref.shape
    tokens = queries_ref.shape[0]
    kv_s[...] = dot(frames_ref[...].reshape(group * frames, width), kv_ref[...]).astype(jnp.bfloat16)
    heads = 4
    span = heads * HEAD_DIM
    lane = lax.broadcasted_iota(jnp.int32, (tokens, span), 1) // HEAD_DIM
    for part in range(width // span):
        lo = part * span
        queries = queries_ref[:, lo : lo + span]
        stacked = jnp.concatenate(
            [jnp.where(lane == h, queries, jnp.zeros_like(queries)) for h in range(heads)], axis=0
        )
        scores = dot(kv_s[:, lo : lo + span], stacked, NT) * SCALE
        scores = scores.reshape(group, frames, heads * tokens)
        weights = jnp.exp(scores - jnp.max(scores, axis=1, keepdims=True))
        weights = (weights / jnp.sum(weights, axis=1, keepdims=True)).astype(jnp.bfloat16)
        for w in range(group):
            rows = slice(w * frames, (w + 1) * frames)
            every = dot(weights[w], kv_s[rows, width + lo : width + lo + span], TN)
            mixed = every[:tokens]
            for h in range(1, heads):
                mixed = jnp.where(lane == h, every[h * tokens : (h + 1) * tokens], mixed)
            ctx_s[w * tokens : (w + 1) * tokens, lo : lo + span] = mixed.astype(jnp.bfloat16)
    projected = dot(ctx_s[...], out_w_ref[...]).reshape(group, tokens, width)
    hidden = queries_ref[...].astype(jnp.float32)[None] + projected
    scale = lax.rsqrt(jnp.mean(hidden * hidden, axis=-1, keepdims=True) + EPSILON)
    mem_s[pl.ds(step * group, group)] = (hidden * scale * gain_ref[...][None]).astype(jnp.bfloat16)

    @pl.when(step == pl.num_programs(0) - 1)
    def _():
        def place(slot, carry):
            packed_ref[slot] = mem_s[index_ref[slot]]
            return carry

        lax.fori_loop(0, packed_ref.shape[0], place, 0)


def compress(index, frames, queries, frame_kv, query_out, gain):
    windows, length, width = frames.shape
    tokens = queries.shape[0]
    slots = index.shape[0]
    group = 8
    whole = lambda *shape: pl.BlockSpec(shape, lambda i, idx: (0,) * len(shape))
    return pl.pallas_call(
        compress_kernel,
        grid_spec=pltpu.PrefetchScalarGridSpec(
            num_scalar_prefetch=1,
            grid=(windows // group,),
            in_specs=[
                pl.BlockSpec((group, length, width), lambda i, idx: (i, 0, 0)),
                whole(tokens, width),
                whole(width, 2 * width),
                whole(width, width),
                whole(1, width),
            ],
            out_specs=whole(slots, tokens, width),
            scratch_shapes=[
                pltpu.VMEM((group * length, 2 * width), jnp.bfloat16),
                pltpu.VMEM((group * tokens, width), jnp.bfloat16),
                pltpu.VMEM((windows, tokens, width), jnp.bfloat16),
            ],
        ),
        out_shape=jax.ShapeDtypeStruct((slots, tokens, width), jnp.bfloat16),
        compiler_params=pltpu.CompilerParams(vmem_limit_bytes=48 * 1024 * 1024),
        cost_estimate=pl.CostEstimate(
            flops=2 * windows * length * width * width * 4,
            bytes_accessed=12 * 1024 * 1024,
            transcendentals=0,
        ),
        name="compress",
    )(index, frames, queries, frame_kv, query_out, gain.reshape(1, width))


def gather_kernel(index_ref, live_ref, table_ref, out_ref):
    def place(row, carry):
        value = table_ref[index_ref[row]]
        out_ref[row] = jnp.where(live_ref[row] > 0, value, jnp.zeros_like(value))
        return carry

    lax.fori_loop(0, out_ref.shape[0], place, 0)


def gather(index, live, table):
    rows = index.shape[0]
    shape = (rows,) + table.shape[1:]
    return pl.pallas_call(
        gather_kernel,
        grid_spec=pltpu.PrefetchScalarGridSpec(
            num_scalar_prefetch=2,
            grid=(1,),
            in_specs=[pl.BlockSpec(table.shape, lambda i, a, b: (0, 0, 0))],
            out_specs=pl.BlockSpec(shape, lambda i, a, b: (0, 0, 0)),
        ),
        out_shape=jax.ShapeDtypeStruct(shape, table.dtype),
        compiler_params=pltpu.CompilerParams(vmem_limit_bytes=24 * 1024 * 1024),
        name="gather",
    )(index, live, table)


def masked_scores(keys, queries, live):
    scores = dot(keys, queries, NT) * SCALE
    token = lax.broadcasted_iota(jnp.int32, scores.shape, 0)
    return jnp.where(token < live, scores, jnp.float32(-1e30))


def stats_kernel(live_ref, q_ref, g_ref, k_ref, v_ref, stats_ref):
    live = live_ref[0]
    rows = []
    for h in range(2):
        scores = masked_scores(k_ref[...], half_lanes(q_ref[...], h), live)
        most = jnp.max(scores, axis=0, keepdims=True)
        weights = jnp.exp(scores - most)
        d_probs = dot(v_ref[...], half_lanes(g_ref[...], h), NT)
        rows += [
            most,
            jnp.sum(weights, axis=0, keepdims=True),
            jnp.sum(weights * d_probs, axis=0, keepdims=True),
        ]
    rows += [jnp.zeros_like(rows[0])] * 2
    stats_ref[0] = jnp.concatenate(rows, axis=0)


def grads_kernel(
    live_ref, q_ref, g_ref, k_ref, v_ref, mine_ref, peer_ref, part_ref, d_kv_ref
):
    live = live_ref[0]
    mine, peer = mine_ref[0], peer_ref[0]
    keys, values = k_ref[...], v_ref[...]
    keys_t, values_t = keys.T, values.T
    d_keys = d_values = None
    d_query, context = [], []
    for h in range(2):
        queries, d_context = half_lanes(q_ref[...], h), half_lanes(g_ref[...], h)
        at = 3 * h
        most = jnp.maximum(mine[at : at + 1], peer[at : at + 1])
        scale_mine = jnp.exp(mine[at : at + 1] - most)
        scale_peer = jnp.exp(peer[at : at + 1] - most)
        inverse = 1.0 / (
            mine[at + 1 : at + 2] * scale_mine + peer[at + 1 : at + 2] * scale_peer
        )
        dots = (
            mine[at + 2 : at + 3] * scale_mine + peer[at + 2 : at + 3] * scale_peer
        ) * inverse
        probs = jnp.exp(masked_scores(keys, queries, live) - most) * inverse
        weights = probs.astype(jnp.bfloat16)
        d_probs = dot(values, d_context, NT)
        d_scores = (probs * (d_probs - dots) * SCALE).astype(jnp.bfloat16)
        cut = slice(h * HEAD_DIM, (h + 1) * HEAD_DIM)
        context.append(dot(values_t[cut], weights))
        d_query.append(dot(keys_t[cut], d_scores))
        dk, dv = dot(d_scores, queries), dot(weights, d_context)
        d_keys = dk if d_keys is None else d_keys + dk
        d_values = dv if d_values is None else d_values + dv
    part_ref[0] = jnp.concatenate(context, axis=0).T.astype(jnp.bfloat16)
    part_ref[1] = jnp.concatenate(d_query, axis=0).T.astype(jnp.bfloat16)
    d_kv_ref[0] = d_keys.astype(jnp.bfloat16)
    d_kv_ref[1] = d_values.astype(jnp.bfloat16)


def attention_specs(rows, keys, pairs):
    column = lambda n, shift: pl.BlockSpec((n, LANES), lambda i, live: (0, i + shift))
    return [column(rows, 0), column(rows, 0), column(keys, 0), column(keys, pairs)]


def attention_stats(live, q, g, kv):
    rows, width = q.shape
    pairs = width // LANES
    return pl.pallas_call(
        stats_kernel,
        grid_spec=pltpu.PrefetchScalarGridSpec(
            num_scalar_prefetch=1,
            grid=(pairs,),
            in_specs=attention_specs(rows, kv.shape[0], pairs),
            out_specs=pl.BlockSpec((1, 8, rows), lambda i, live: (i, 0, 0)),
        ),
        out_shape=jax.ShapeDtypeStruct((pairs, 8, rows), jnp.float32),
        compiler_params=pltpu.CompilerParams(vmem_limit_bytes=32 * 1024 * 1024),
        name="attention_stats",
    )(live, q, g, kv, kv)


def attention_grads(live, q, g, kv, mine, peer):
    rows, width = q.shape
    keys = kv.shape[0]
    pairs = width // LANES
    stats = pl.BlockSpec((1, 8, rows), lambda i, live: (i, 0, 0))
    return pl.pallas_call(
        grads_kernel,
        grid_spec=pltpu.PrefetchScalarGridSpec(
            num_scalar_prefetch=1,
            grid=(pairs,),
            in_specs=attention_specs(rows, keys, pairs) + [stats, stats],
            out_specs=[
                pl.BlockSpec((2, rows, LANES), lambda i, live: (0, 0, i)),
                pl.BlockSpec((2, keys, LANES), lambda i, live: (0, 0, i)),
            ],
        ),
        out_shape=[
            jax.ShapeDtypeStruct((2, rows, width), jnp.bfloat16),
            jax.ShapeDtypeStruct((2, keys, width), jnp.bfloat16),
        ],
        compiler_params=pltpu.CompilerParams(vmem_limit_bytes=32 * 1024 * 1024),
        name="attention_grads",
    )(live, q, g, kv, kv, mine, peer)


def halving_orders(bits):
    middle = list(range(bits - 1, 0, -1))
    return [bits, 0] + middle, [bits] + middle[:1] + [0] + middle[1:]


def tail_kernel(
    bits,
    return_ref,
    target_ref,
    half_ref,
    d_kv_ref,
    memory_kv_ref,
    part_ref,
    x_ref,
    grad_out_ref,
    gain_ref,
    w_query_ref,
    w_output_ref,
    kv_grad_ref,
    memory_grad_ref,
    decoded_ref,
    caption_grad_ref,
    *scratch,
):
    mesh_ids = pl.DeviceIdType.MESH
    stages = bits + 1
    n_dev = 2**bits
    got, held = scratch[: 2 * stages], scratch[2 * stages : 4 * stages - 2]
    terms = scratch[4 * stages - 2 : 4 * stages]
    (d_mem, slots, returned, other_part, w_query_s, w_output_s, send_sem, recv_sem,
     slot_send, slot_recv, part_sem, load_sem) = scratch[4 * stages :]
    section, dev = lax.axis_index("section"), lax.axis_index("dev")
    mine = [section] + [lax.rem(dev // 2 ** (bits - t), 2) for t in range(1, bits + 1)]
    peers = [(1 - section, dev)] + [
        (section, dev + (1 - 2 * mine[t]) * 2 ** (bits - t)) for t in range(1, bits + 1)
    ]
    loads = [
        pltpu.make_async_copy(w_query_ref, w_query_s, load_sem.at[0]),
        pltpu.make_async_copy(w_output_ref, w_output_s, load_sem.at[1]),
    ]
    for load in loads:
        load.start()
    barrier = pltpu.get_barrier_semaphore()
    pl.semaphore_signal(barrier, inc=1, device_id=peers[0], device_id_type=mesh_ids)

    def greet(k, carry):
        peer = (section, lax.rem(dev + k, n_dev))
        pl.semaphore_signal(barrier, inc=1, device_id=peer, device_id_type=mesh_ids)
        return carry

    lax.fori_loop(1, n_dev, greet, 0)

    width = half_ref.shape[1]
    inner = d_kv_ref.shape[2]
    chunk = width // 4

    def memory_columns(j, carry):
        at = pl.ds(pl.multiple_of(j * chunk, chunk), chunk)
        value = dot(d_kv_ref[0], memory_kv_ref[at, :inner], NT)
        value = value + dot(d_kv_ref[1], memory_kv_ref[at, inner:], NT)
        d_mem[:, :, at] = value.astype(jnp.bfloat16).reshape(d_mem.shape[:2] + (chunk,))
        return carry

    lax.fori_loop(0, 4, memory_columns, 0)
    per_slot = slots.shape[1]

    def pack(i, carry):
        slots[i // per_slot, lax.rem(i, per_slot)] = d_mem[return_ref[i]]
        return carry

    lax.fori_loop(0, n_dev * per_slot, pack, 0)
    pl.semaphore_wait(barrier, n_dev)

    def slot_copy(k):
        to = lax.rem(dev + k, n_dev)
        return pltpu.make_async_remote_copy(
            src_ref=slots.at[to],
            dst_ref=returned.at[dev],
            send_sem=slot_send.at[k],
            recv_sem=slot_recv.at[k],
            device_id=(section, to),
            device_id_type=mesh_ids,
        )

    caplen = x_ref.shape[0]
    part_copy = pltpu.make_async_remote_copy(
        src_ref=part_ref.at[:, pl.ds(caplen, caplen)],
        dst_ref=other_part,
        send_sem=part_sem.at[0],
        recv_sem=part_sem.at[1],
        device_id=peers[0],
        device_id_type=mesh_ids,
    )
    part_copy.start()

    def send_slot(i, carry):
        slot_copy(lax.rem(i + n_dev // 2 - 1, n_dev - 1) + 1).start()
        return carry

    lax.fori_loop(0, n_dev - 1, send_slot, 0)
    returned[dev] = slots[dev]

    for c in range(2):

        def term_rows(j, carry):
            at = pl.ds(pl.multiple_of(j * chunk, chunk), chunk)
            value = dot(half_ref[:, at], d_kv_ref[c], TN).astype(jnp.bfloat16)
            terms[c][j // 2, lax.rem(j, 2)] = value.reshape(terms[c].shape[2:])
            return carry

        lax.fori_loop(0, 4, term_rows, 0)

    orders = halving_orders(bits)

    def source(chain, stage):
        return terms[chain] if stage == 0 else held[chain * (stages - 1) + stage - 1]

    def place(chain, stage):
        done = orders[chain][:stage]
        return sum(1 for t in range(orders[chain][stage]) if t not in done)

    def copy(chain, stage):
        at = (slice(None),) * place(chain, stage)
        t = orders[chain][stage]
        return pltpu.make_async_remote_copy(
            src_ref=source(chain, stage).at[at + (1 - mine[t],)],
            dst_ref=got[chain * stages + stage],
            send_sem=send_sem.at[chain * stages + stage],
            recv_sem=recv_sem.at[chain * stages + stage],
            device_id=peers[t],
            device_id_type=mesh_ids,
        )

    copies = {(c, 0): copy(c, 0) for c in range(2)}
    for c in range(2):
        copies[c, 0].start()
    for stage in range(stages):
        for c in range(2):
            copies[c, stage].wait_recv()
            left = stages - 1 - stage
            at, bit = place(c, stage), mine[orders[c][stage]]
            src, other = source(c, stage), got[c * stages + stage]

            def add(i, carry):
                index = tuple(lax.rem(i // 2 ** (left - 1 - n), 2) for n in range(left))
                total = src[index[:at] + (bit,) + index[at:]].astype(jnp.float32)
                total = total + other[index].astype(jnp.float32)
                if left:
                    held[c * (stages - 1) + stage][index] = total.astype(jnp.bfloat16)
                else:
                    kv_grad_ref[:, c * inner : (c + 1) * inner] = total
                return carry

            if left:
                lax.fori_loop(0, 2**left, add, 0)
                copies[c, stage + 1] = copy(c, stage + 1)
                copies[c, stage + 1].start()
            else:
                add(0, 0)
        if stage == 0:
            part_copy.wait_recv()
            for load in loads:
                load.wait()
            merged = [
                (
                    part_ref[n, :caplen, :].astype(jnp.float32) + other_part[n].astype(jnp.float32)
                ).astype(jnp.bfloat16)
                for n in range(2)
            ]
            x = x_ref[...].astype(jnp.float32)
            decoded_ref[...] = (x + dot(merged[0], w_output_s[...])).astype(jnp.bfloat16)
            inv_rms = lax.rsqrt(jnp.mean(x * x, axis=-1, keepdims=True) + EPSILON)
            d_scaled = dot(merged[1], w_query_s[...], NT) * gain_ref[...]
            mean = jnp.mean(d_scaled * x, axis=-1, keepdims=True)
            caption_grad_ref[...] = (
                grad_out_ref[...].astype(jnp.float32)
                + inv_rms * (d_scaled - x * inv_rms * inv_rms * mean)
            ).astype(jnp.bfloat16)

    def arrive(k, carry):
        slot_copy(k).wait_recv()
        return carry

    lax.fori_loop(1, n_dev, arrive, 0)

    def unpack(j, carry):
        memory_grad_ref[j] = returned[target_ref[j] // per_slot, lax.rem(target_ref[j], per_slot)]
        return carry

    lax.fori_loop(0, memory_grad_ref.shape[0], unpack, 0)

    def sent(k, carry):
        slot_copy(k).wait_send()
        return carry

    lax.fori_loop(1, n_dev, sent, 0)
    part_copy.wait_send()
    for made in copies.values():
        made.wait_send()


def tail(return_index, target, half, d_kv, memory_kv, part, x, grad_out, gain, w_query, w_output):
    n_section, n_dev = lax.axis_size("section"), lax.axis_size("dev")
    bits = n_dev.bit_length() - 1
    stages = bits + 1
    width, inner = half.shape[1], d_kv.shape[2]
    rows = width // (n_section * n_dev)
    caplen, model = x.shape
    slots = (n_dev, return_index.shape[0] // n_dev, half.shape[0] // MOST_WIN, width)
    bf16 = jnp.bfloat16
    block = lambda n: pltpu.VMEM((2,) * n + (rows, inner), bf16)
    vmem = pl.BlockSpec(memory_space=pltpu.VMEM)
    smem = pl.BlockSpec(memory_space=pltpu.SMEM)
    far = pl.BlockSpec(memory_space=pl.ANY)
    dma = pltpu.SemaphoreType.DMA
    return pl.pallas_call(
        functools.partial(tail_kernel, bits),
        out_shape=[
            jax.ShapeDtypeStruct((rows, 2 * inner), jnp.float32),
            jax.ShapeDtypeStruct((target.shape[0],) + slots[2:], bf16),
            jax.ShapeDtypeStruct((caplen, model), bf16),
            jax.ShapeDtypeStruct((caplen, model), bf16),
        ],
        in_specs=[smem] * 2 + [vmem] * 7 + [far] * 2,
        out_specs=[vmem] * 4,
        scratch_shapes=[block(stages - 1 - s) for _ in range(2) for s in range(stages)]
        + [block(stages - 1 - s) for _ in range(2) for s in range(stages - 1)]
        + [block(stages)] * 2
        + [
            pltpu.VMEM((MOST_WIN,) + slots[2:], bf16),
            pltpu.VMEM(slots, bf16),
            pltpu.VMEM(slots, bf16),
            pltpu.VMEM((2, caplen, inner), bf16),
            pltpu.VMEM(w_query.shape, bf16),
            pltpu.VMEM(w_output.shape, bf16),
            dma((2 * stages,)),
            dma((2 * stages,)),
            dma((n_dev,)),
            dma((n_dev,)),
            dma((2,)),
            dma((2,)),
        ],
        compiler_params=pltpu.CompilerParams(
            collective_id=0, has_side_effects=True, vmem_limit_bytes=48 * 1024 * 1024
        ),
        name="tail",
    )(
        return_index, target, half, d_kv, memory_kv, part, x, grad_out,
        gain.reshape(1, model), w_query, w_output,
    )


def swap(x):
    return lax.ppermute(x, "section", [(0, 1), (1, 0)])


def local(
    frames,
    window_counts,
    learned_queries,
    frame_kv,
    query_out,
    query_gain,
    captions,
    caption_lengths,
    caption_gain,
    w_query,
    memory_kv,
    w_output,
    upstream,
):
    videos = lax.axis_size("dev")
    windows, _, width = frames.shape
    tokens = learned_queries.shape[0]
    inner = w_query.shape[1]
    caplen = captions.shape[2]
    per_slot = (MOST_WIN + videos - 2) // (videos - 1)
    section_id = lax.axis_index("section")
    video_id = lax.axis_index("dev")
    counts_row = lax.dynamic_index_in_dim(window_counts, section_id, 0, keepdims=False)
    run_ends = jnp.cumsum(counts_row)
    starts = run_ends - counts_row
    local_index = jnp.arange(windows, dtype=jnp.int32)
    ranked = (
        local_index // per_slot * (per_slot * videos) + video_id * per_slot + local_index % per_slot
    )
    owner_video = jnp.sum((run_ends[None, :] <= ranked[:, None]).astype(jnp.int32), axis=1)
    target = owner_video * per_slot + local_index % per_slot
    slot_index = jnp.arange(videos * per_slot, dtype=jnp.int32)
    send_index = jnp.sum(
        jnp.where(slot_index[:, None] == target[None, :], local_index[None, :], 0), axis=1
    )
    count_here = lax.dynamic_index_in_dim(counts_row, video_id, 0, keepdims=False)
    start_here = lax.dynamic_index_in_dim(starts, video_id, 0, keepdims=False)
    position = jnp.arange(MOST_WIN, dtype=jnp.int32)
    incoming = start_here + position
    source_slot = incoming // per_slot % videos * per_slot + incoming % per_slot
    present = position < count_here
    return_index = jnp.sum(
        jnp.where(
            (slot_index[:, None] == source_slot[None, :]) & present[None, :], position[None, :], 0
        ),
        axis=1,
    )
    live = (count_here * tokens).reshape(1)

    x = captions[0, 0].astype(jnp.float32)
    inv_rms = lax.rsqrt(jnp.mean(x * x, axis=-1, keepdims=True) + EPSILON)
    normed = (x * inv_rms * caption_gain).astype(jnp.bfloat16)
    query = dot(normed, w_query).astype(jnp.bfloat16)
    row_live = jnp.arange(caplen, dtype=jnp.int32) < caption_lengths[0, 0]
    grad_out = jnp.where(row_live[:, None], upstream[0, 0], jnp.zeros_like(upstream[0, 0]))
    d_context = dot(grad_out, w_output, NT).astype(jnp.bfloat16)
    own = jnp.stack([query, d_context])
    both = jnp.concatenate([own, swap(own)], axis=1)

    packed = compress(send_index, frames, learned_queries, frame_kv, query_out, query_gain)
    arrived = lax.all_to_all(
        packed.reshape(videos, per_slot, tokens, width), "dev", split_axis=0, concat_axis=0, tiled=True
    ).reshape(videos * per_slot, tokens, width)
    memory_half = gather(source_slot, present.astype(jnp.int32), arrived).reshape(
        MOST_WIN * tokens, width
    )
    key_value = dot(memory_half, memory_kv).astype(jnp.bfloat16)

    stats = attention_stats(live, both[0], both[1], key_value)
    peer = swap(stats)
    peer = jnp.concatenate([peer[..., caplen:], peer[..., :caplen]], axis=-1)
    partial, d_kv = attention_grads(live, both[0], both[1], key_value, stats, peer)

    kv_grad, memory_grad, decoded, caption_grad = tail(
        return_index,
        target,
        memory_half,
        d_kv,
        memory_kv,
        partial,
        captions[0, 0],
        grad_out,
        caption_gain,
        w_query,
        w_output,
    )
    return decoded[None, None], caption_grad[None, None], memory_grad, kv_grad


def solution(mesh):
    return jax.shard_map(
        local,
        mesh=mesh,
        in_specs=(
            P(("section", "dev"), None, None),
            P(),
            P(),
            P(),
            P(),
            P(),
            P("section", "dev", None, None),
            P("section", "dev"),
            P(),
            P(),
            P(),
            P(),
            P("section", "dev", None, None),
        ),
        out_specs=(
            P("section", "dev", None, None),
            P("section", "dev", None, None),
            P(("section", "dev"), None, None),
            P(("section", "dev"), None),
        ),
        check_vma=False,
    )
```

```python
import functools

import jax
import jax.numpy as jnp
from jax import lax
from jax.experimental import pallas as pl
from jax.experimental.pallas import tpu as pltpu
from jax.sharding import PartitionSpec as P

HEAD_DIM = 64
MOST_WIN = 20
EPSILON = 1e-06
SCALE = HEAD_DIM ** (-0.5)
NT = (((1,), (1,)), ((), ()))
TN = (((0,), (0,)), ((), ()))
LANES = 128


def dot(a, b, dims=(((1,), (0,)), ((), ()))):
    return lax.dot_general(a, b, dims, preferred_element_type=jnp.float32)


def half_lanes(x, which):
    lane = lax.broadcasted_iota(jnp.int32, x.shape, 1)
    return jnp.where(lane // HEAD_DIM == which, x, jnp.zeros_like(x))


def head_kernel(
    send_ref, source_ref, frames_ref, queries_ref, frame_kv_ref, query_out_ref, gain_ref,
    normed_ref, grad_out_ref, w_query_ref, w_output_ref, memory_kv_ref,
    both_ref, half_ref, keys_ref,
    kv_s, ctx_s, mem_s, slots, arrived, own, swapped, w_query_s, w_output_s, memory_kv_s,
    slot_send, slot_recv, swap_sem, load_sem,
):
    mesh_ids = pl.DeviceIdType.MESH
    section, dev = lax.axis_index("section"), lax.axis_index("dev")
    n_dev, per_slot = slots.shape[:2]
    loads = [
        pltpu.make_async_copy(src, dst, load_sem.at[n])
        for n, (src, dst) in enumerate(
            ((w_query_ref, w_query_s), (w_output_ref, w_output_s), (memory_kv_ref, memory_kv_s))
        )
    ]
    for load in loads:
        load.start()
    barrier = pltpu.get_barrier_semaphore()
    peer = (1 - section, dev)
    pl.semaphore_signal(barrier, inc=1, device_id=peer, device_id_type=mesh_ids)

    def greet(k, carry):
        to = (section, lax.rem(dev + k, n_dev))
        pl.semaphore_signal(barrier, inc=1, device_id=to, device_id_type=mesh_ids)
        return carry

    lax.fori_loop(1, n_dev, greet, 0)
    windows, frames, width = frames_ref.shape
    tokens = queries_ref.shape[0]
    group = kv_s.shape[0] // frames

    def compress(step, carry):
        block = frames_ref[pl.ds(step * group, group)].reshape(group * frames, width)
        kv_s[...] = dot(block, frame_kv_ref[...]).astype(jnp.bfloat16)
        heads = 4
        span = heads * HEAD_DIM
        lane = lax.broadcasted_iota(jnp.int32, (tokens, span), 1) // HEAD_DIM
        for part in range(width // span):
            lo = part * span
            queries = queries_ref[:, lo : lo + span]
            stacked = jnp.concatenate(
                [jnp.where(lane == h, queries, jnp.zeros_like(queries)) for h in range(heads)], axis=0
            )
            scores = dot(kv_s[:, lo : lo + span], stacked, NT) * SCALE
            scores = scores.reshape(group, frames, heads * tokens)
            weights = jnp.exp(scores - jnp.max(scores, axis=1, keepdims=True))
            weights = (weights / jnp.sum(weights, axis=1, keepdims=True)).astype(jnp.bfloat16)
            for w in range(group):
                rows = slice(w * frames, (w + 1) * frames)
                every = dot(weights[w], kv_s[rows, width + lo : width + lo + span], TN)
                mixed = every[:tokens]
                for h in range(1, heads):
                    mixed = jnp.where(lane == h, every[h * tokens : (h + 1) * tokens], mixed)
                ctx_s[w * tokens : (w + 1) * tokens, lo : lo + span] = mixed.astype(jnp.bfloat16)
        projected = dot(ctx_s[...], query_out_ref[...]).reshape(group, tokens, width)
        hidden = queries_ref[...].astype(jnp.float32)[None] + projected
        scale = lax.rsqrt(jnp.mean(hidden * hidden, axis=-1, keepdims=True) + EPSILON)
        memory = hidden * scale * gain_ref[...][None]
        mem_s[pl.ds(step * group, group)] = memory.astype(jnp.bfloat16)
        return carry

    lax.fori_loop(0, windows // group, compress, 0)

    def pack(i, carry):
        slots[i // per_slot, lax.rem(i, per_slot)] = mem_s[send_ref[i]]
        return carry

    lax.fori_loop(0, n_dev * per_slot, pack, 0)
    pl.semaphore_wait(barrier, n_dev)

    def slot_copy(k):
        to = lax.rem(dev + k, n_dev)
        return pltpu.make_async_remote_copy(
            src_ref=slots.at[to],
            dst_ref=arrived.at[dev],
            send_sem=slot_send.at[k],
            recv_sem=slot_recv.at[k],
            device_id=(section, to),
            device_id_type=mesh_ids,
        )

    def send_slot(i, carry):
        slot_copy(lax.rem(i + n_dev // 2 - 1, n_dev - 1) + 1).start()
        return carry

    lax.fori_loop(0, n_dev - 1, send_slot, 0)
    arrived[dev] = slots[dev]
    for load in loads:
        load.wait()
    caplen = normed_ref.shape[0]
    own[0] = dot(normed_ref[...], w_query_s[...]).astype(jnp.bfloat16)
    own[1] = dot(grad_out_ref[...], w_output_s[...], NT).astype(jnp.bfloat16)
    both_ref[:, :caplen, :] = own[...]
    swap_copy = pltpu.make_async_remote_copy(
        src_ref=own,
        dst_ref=swapped,
        send_sem=swap_sem.at[0],
        recv_sem=swap_sem.at[1],
        device_id=peer,
        device_id_type=mesh_ids,
    )
    swap_copy.start()
    swap_copy.wait_recv()
    both_ref[:, caplen:, :] = swapped[...]

    def arrive(k, carry):
        slot_copy(k).wait_recv()
        return carry

    lax.fori_loop(1, n_dev, arrive, 0)

    def take(p, carry):
        at = source_ref[p]
        rows = pl.ds(pl.multiple_of(p * tokens, tokens), tokens)
        half_ref[rows, :] = arrived[at // per_slot, lax.rem(at, per_slot)]
        return carry

    lax.fori_loop(0, half_ref.shape[0] // tokens, take, 0)
    chunk = memory_kv_s.shape[1] // 4

    def project(j, carry):
        at = pl.ds(pl.multiple_of(j * chunk, chunk), chunk)
        keys_ref[:, at] = dot(half_ref[...], memory_kv_s[:, at]).astype(jnp.bfloat16)
        return carry

    lax.fori_loop(0, 4, project, 0)

    def sent(k, carry):
        slot_copy(k).wait_send()
        return carry

    lax.fori_loop(1, n_dev, sent, 0)
    swap_copy.wait_send()


def head(
    send_index, source_slot, frames, queries, frame_kv, query_out, gain,
    normed, grad_out, w_query, w_output, memory_kv,
):
    n_dev = lax.axis_size("dev")
    windows, length, width = frames.shape
    tokens = queries.shape[0]
    caplen, inner = normed.shape[0], w_query.shape[1]
    keys = MOST_WIN * tokens
    slots = (n_dev, send_index.shape[0] // n_dev, tokens, width)
    group = 8
    bf16 = jnp.bfloat16
    vmem = pl.BlockSpec(memory_space=pltpu.VMEM)
    smem = pl.BlockSpec(memory_space=pltpu.SMEM)
    far = pl.BlockSpec(memory_space=pl.ANY)
    dma = pltpu.SemaphoreType.DMA
    shapes = [
        (group * length, 2 * width),
        (group * tokens, width),
        (windows, tokens, width),
        slots,
        slots,
        (2, caplen, inner),
        (2, caplen, inner),
        w_query.shape,
        w_output.shape,
        memory_kv.shape,
    ]
    return pl.pallas_call(
        head_kernel,
        out_shape=[
            jax.ShapeDtypeStruct((2, 2 * caplen, inner), bf16),
            jax.ShapeDtypeStruct((keys, width), bf16),
            jax.ShapeDtypeStruct((keys, memory_kv.shape[1]), bf16),
        ],
        in_specs=[smem] * 2 + [vmem] * 7 + [far] * 3,
        out_specs=[vmem] * 3,
        scratch_shapes=[pltpu.VMEM(shape, bf16) for shape in shapes]
        + [dma((n_dev,)), dma((n_dev,)), dma((2,)), dma((3,))],
        compiler_params=pltpu.CompilerParams(
            collective_id=1, has_side_effects=True, vmem_limit_bytes=40 * 1024 * 1024
        ),
        name="head",
    )(
        send_index, source_slot, frames, queries, frame_kv, query_out, gain.reshape(1, width),
        normed, grad_out, w_query, w_output, memory_kv,
    )


def masked_scores(keys, queries, live):
    scores = dot(keys, queries, NT) * SCALE
    token = lax.broadcasted_iota(jnp.int32, scores.shape, 0)
    return jnp.where(token < live, scores, jnp.float32(-1e30))


def stats_kernel(live_ref, q_ref, g_ref, k_ref, v_ref, stats_ref):
    live = live_ref[0]
    rows = []
    for h in range(2):
        scores = masked_scores(k_ref[...], half_lanes(q_ref[...], h), live)
        most = jnp.max(scores, axis=0, keepdims=True)
        weights = jnp.exp(scores - most)
        d_probs = dot(v_ref[...], half_lanes(g_ref[...], h), NT)
        rows += [
            most,
            jnp.sum(weights, axis=0, keepdims=True),
            jnp.sum(weights * d_probs, axis=0, keepdims=True),
        ]
    rows += [jnp.zeros_like(rows[0])] * 2
    stats_ref[0] = jnp.concatenate(rows, axis=0)


def grads_kernel(
    live_ref, q_ref, g_ref, k_ref, v_ref, mine_ref, peer_ref, part_ref, d_kv_ref
):
    live = live_ref[0]
    mine, peer = mine_ref[0], peer_ref[0]
    keys, values = k_ref[...], v_ref[...]
    keys_t, values_t = keys.T, values.T
    d_keys = d_values = None
    d_query, context = [], []
    for h in range(2):
        queries, d_context = half_lanes(q_ref[...], h), half_lanes(g_ref[...], h)
        at = 3 * h
        most = jnp.maximum(mine[at : at + 1], peer[at : at + 1])
        scale_mine = jnp.exp(mine[at : at + 1] - most)
        scale_peer = jnp.exp(peer[at : at + 1] - most)
        inverse = 1.0 / (
            mine[at + 1 : at + 2] * scale_mine + peer[at + 1 : at + 2] * scale_peer
        )
        dots = (
            mine[at + 2 : at + 3] * scale_mine + peer[at + 2 : at + 3] * scale_peer
        ) * inverse
        probs = jnp.exp(masked_scores(keys, queries, live) - most) * inverse
        weights = probs.astype(jnp.bfloat16)
        d_probs = dot(values, d_context, NT)
        d_scores = (probs * (d_probs - dots) * SCALE).astype(jnp.bfloat16)
        cut = slice(h * HEAD_DIM, (h + 1) * HEAD_DIM)
        context.append(dot(values_t[cut], weights))
        d_query.append(dot(keys_t[cut], d_scores))
        dk, dv = dot(d_scores, queries), dot(weights, d_context)
        d_keys = dk if d_keys is None else d_keys + dk
        d_values = dv if d_values is None else d_values + dv
    part_ref[0] = jnp.concatenate(context, axis=0).T.astype(jnp.bfloat16)
    part_ref[1] = jnp.concatenate(d_query, axis=0).T.astype(jnp.bfloat16)
    d_kv_ref[0] = d_keys.astype(jnp.bfloat16)
    d_kv_ref[1] = d_values.astype(jnp.bfloat16)


def attention_specs(rows, keys, pairs):
    column = lambda n, shift: pl.BlockSpec((n, LANES), lambda i, live: (0, i + shift))
    return [column(rows, 0), column(rows, 0), column(keys, 0), column(keys, pairs)]


def attention_stats(live, q, g, kv):
    rows, width = q.shape
    pairs = width // LANES
    return pl.pallas_call(
        stats_kernel,
        grid_spec=pltpu.PrefetchScalarGridSpec(
            num_scalar_prefetch=1,
            grid=(pairs,),
            in_specs=attention_specs(rows, kv.shape[0], pairs),
            out_specs=pl.BlockSpec((1, 8, rows), lambda i, live: (i, 0, 0)),
        ),
        out_shape=jax.ShapeDtypeStruct((pairs, 8, rows), jnp.float32),
        compiler_params=pltpu.CompilerParams(vmem_limit_bytes=32 * 1024 * 1024),
        name="attention_stats",
    )(live, q, g, kv, kv)


def attention_grads(live, q, g, kv, mine, peer):
    rows, width = q.shape
    keys = kv.shape[0]
    pairs = width // LANES
    stats = pl.BlockSpec((1, 8, rows), lambda i, live: (i, 0, 0))
    return pl.pallas_call(
        grads_kernel,
        grid_spec=pltpu.PrefetchScalarGridSpec(
            num_scalar_prefetch=1,
            grid=(pairs,),
            in_specs=attention_specs(rows, keys, pairs) + [stats, stats],
            out_specs=[
                pl.BlockSpec((2, rows, LANES), lambda i, live: (0, 0, i)),
                pl.BlockSpec((2, keys, LANES), lambda i, live: (0, 0, i)),
            ],
        ),
        out_shape=[
            jax.ShapeDtypeStruct((2, rows, width), jnp.bfloat16),
            jax.ShapeDtypeStruct((2, keys, width), jnp.bfloat16),
        ],
        compiler_params=pltpu.CompilerParams(vmem_limit_bytes=32 * 1024 * 1024),
        name="attention_grads",
    )(live, q, g, kv, kv, mine, peer)


def halving_orders(bits):
    middle = list(range(bits - 1, 0, -1))
    return [bits, 0] + middle, [bits] + middle[:1] + [0] + middle[1:]


def tail_kernel(
    bits,
    return_ref,
    target_ref,
    half_ref,
    d_kv_ref,
    memory_kv_ref,
    part_ref,
    x_ref,
    grad_out_ref,
    gain_ref,
    w_query_ref,
    w_output_ref,
    kv_grad_ref,
    memory_grad_ref,
    decoded_ref,
    caption_grad_ref,
    *scratch,
):
    mesh_ids = pl.DeviceIdType.MESH
    stages = bits + 1
    n_dev = 2**bits
    got, held = scratch[: 2 * stages], scratch[2 * stages : 4 * stages - 2]
    terms = scratch[4 * stages - 2 : 4 * stages]
    (d_mem, slots, returned, other_part, w_query_s, w_output_s, send_sem, recv_sem,
     slot_send, slot_recv, part_sem, load_sem) = scratch[4 * stages :]
    section, dev = lax.axis_index("section"), lax.axis_index("dev")
    mine = [section] + [lax.rem(dev // 2 ** (bits - t), 2) for t in range(1, bits + 1)]
    peers = [(1 - section, dev)] + [
        (section, dev + (1 - 2 * mine[t]) * 2 ** (bits - t)) for t in range(1, bits + 1)
    ]
    loads = [
        pltpu.make_async_copy(w_query_ref, w_query_s, load_sem.at[0]),
        pltpu.make_async_copy(w_output_ref, w_output_s, load_sem.at[1]),
    ]
    for load in loads:
        load.start()
    barrier = pltpu.get_barrier_semaphore()
    pl.semaphore_signal(barrier, inc=1, device_id=peers[0], device_id_type=mesh_ids)

    def greet(k, carry):
        peer = (section, lax.rem(dev + k, n_dev))
        pl.semaphore_signal(barrier, inc=1, device_id=peer, device_id_type=mesh_ids)
        return carry

    lax.fori_loop(1, n_dev, greet, 0)

    width = half_ref.shape[1]
    inner = d_kv_ref.shape[2]
    chunk = width // 4

    def memory_columns(j, carry):
        at = pl.ds(pl.multiple_of(j * chunk, chunk), chunk)
        value = dot(d_kv_ref[0], memory_kv_ref[at, :inner], NT)
        value = value + dot(d_kv_ref[1], memory_kv_ref[at, inner:], NT)
        d_mem[:, :, at] = value.astype(jnp.bfloat16).reshape(d_mem.shape[:2] + (chunk,))
        return carry

    lax.fori_loop(0, 4, memory_columns, 0)
    per_slot = slots.shape[1]

    def pack(i, carry):
        slots[i // per_slot, lax.rem(i, per_slot)] = d_mem[return_ref[i]]
        return carry

    lax.fori_loop(0, n_dev * per_slot, pack, 0)
    pl.semaphore_wait(barrier, n_dev)

    def slot_copy(k):
        to = lax.rem(dev + k, n_dev)
        return pltpu.make_async_remote_copy(
            src_ref=slots.at[to],
            dst_ref=returned.at[dev],
            send_sem=slot_send.at[k],
            recv_sem=slot_recv.at[k],
            device_id=(section, to),
            device_id_type=mesh_ids,
        )

    caplen = x_ref.shape[0]
    part_copy = pltpu.make_async_remote_copy(
        src_ref=part_ref.at[:, pl.ds(caplen, caplen)],
        dst_ref=other_part,
        send_sem=part_sem.at[0],
        recv_sem=part_sem.at[1],
        device_id=peers[0],
        device_id_type=mesh_ids,
    )
    part_copy.start()

    def send_slot(i, carry):
        slot_copy(lax.rem(i + n_dev // 2 - 1, n_dev - 1) + 1).start()
        return carry

    lax.fori_loop(0, n_dev - 1, send_slot, 0)
    returned[dev] = slots[dev]

    for c in range(2):

        def term_rows(j, carry):
            at = pl.ds(pl.multiple_of(j * chunk, chunk), chunk)
            value = dot(half_ref[:, at], d_kv_ref[c], TN).astype(jnp.bfloat16)
            terms[c][j // 2, lax.rem(j, 2)] = value.reshape(terms[c].shape[2:])
            return carry

        lax.fori_loop(0, 4, term_rows, 0)

    orders = halving_orders(bits)

    def source(chain, stage):
        return terms[chain] if stage == 0 else held[chain * (stages - 1) + stage - 1]

    def place(chain, stage):
        done = orders[chain][:stage]
        return sum(1 for t in range(orders[chain][stage]) if t not in done)

    def copy(chain, stage):
        at = (slice(None),) * place(chain, stage)
        t = orders[chain][stage]
        return pltpu.make_async_remote_copy(
            src_ref=source(chain, stage).at[at + (1 - mine[t],)],
            dst_ref=got[chain * stages + stage],
            send_sem=send_sem.at[chain * stages + stage],
            recv_sem=recv_sem.at[chain * stages + stage],
            device_id=peers[t],
            device_id_type=mesh_ids,
        )

    copies = {(c, 0): copy(c, 0) for c in range(2)}
    for c in range(2):
        copies[c, 0].start()
    for stage in range(stages):
        for c in range(2):
            copies[c, stage].wait_recv()
            left = stages - 1 - stage
            at, bit = place(c, stage), mine[orders[c][stage]]
            src, other = source(c, stage), got[c * stages + stage]

            def add(i, carry):
                index = tuple(lax.rem(i // 2 ** (left - 1 - n), 2) for n in range(left))
                total = src[index[:at] + (bit,) + index[at:]].astype(jnp.float32)
                total = total + other[index].astype(jnp.float32)
                if left:
                    held[c * (stages - 1) + stage][index] = total.astype(jnp.bfloat16)
                else:
                    kv_grad_ref[:, c * inner : (c + 1) * inner] = total
                return carry

            if left:
                lax.fori_loop(0, 2**left, add, 0)
                copies[c, stage + 1] = copy(c, stage + 1)
                copies[c, stage + 1].start()
            else:
                add(0, 0)
        if stage == 0:
            part_copy.wait_recv()
            for load in loads:
                load.wait()
            merged = [
                (
                    part_ref[n, :caplen, :].astype(jnp.float32) + other_part[n].astype(jnp.float32)
                ).astype(jnp.bfloat16)
                for n in range(2)
            ]
            x = x_ref[...].astype(jnp.float32)
            decoded_ref[...] = (x + dot(merged[0], w_output_s[...])).astype(jnp.bfloat16)
            inv_rms = lax.rsqrt(jnp.mean(x * x, axis=-1, keepdims=True) + EPSILON)
            d_scaled = dot(merged[1], w_query_s[...], NT) * gain_ref[...]
            mean = jnp.mean(d_scaled * x, axis=-1, keepdims=True)
            caption_grad_ref[...] = (
                grad_out_ref[...].astype(jnp.float32)
                + inv_rms * (d_scaled - x * inv_rms * inv_rms * mean)
            ).astype(jnp.bfloat16)

    def arrive(k, carry):
        slot_copy(k).wait_recv()
        return carry

    lax.fori_loop(1, n_dev, arrive, 0)

    def unpack(j, carry):
        memory_grad_ref[j] = returned[target_ref[j] // per_slot, lax.rem(target_ref[j], per_slot)]
        return carry

    lax.fori_loop(0, memory_grad_ref.shape[0], unpack, 0)

    def sent(k, carry):
        slot_copy(k).wait_send()
        return carry

    lax.fori_loop(1, n_dev, sent, 0)
    part_copy.wait_send()
    for made in copies.values():
        made.wait_send()


def tail(return_index, target, half, d_kv, memory_kv, part, x, grad_out, gain, w_query, w_output):
    n_section, n_dev = lax.axis_size("section"), lax.axis_size("dev")
    bits = n_dev.bit_length() - 1
    stages = bits + 1
    width, inner = half.shape[1], d_kv.shape[2]
    rows = width // (n_section * n_dev)
    caplen, model = x.shape
    slots = (n_dev, return_index.shape[0] // n_dev, half.shape[0] // MOST_WIN, width)
    bf16 = jnp.bfloat16
    block = lambda n: pltpu.VMEM((2,) * n + (rows, inner), bf16)
    vmem = pl.BlockSpec(memory_space=pltpu.VMEM)
    smem = pl.BlockSpec(memory_space=pltpu.SMEM)
    far = pl.BlockSpec(memory_space=pl.ANY)
    dma = pltpu.SemaphoreType.DMA
    return pl.pallas_call(
        functools.partial(tail_kernel, bits),
        out_shape=[
            jax.ShapeDtypeStruct((rows, 2 * inner), jnp.float32),
            jax.ShapeDtypeStruct((target.shape[0],) + slots[2:], bf16),
            jax.ShapeDtypeStruct((caplen, model), bf16),
            jax.ShapeDtypeStruct((caplen, model), bf16),
        ],
        in_specs=[smem] * 2 + [vmem] * 7 + [far] * 2,
        out_specs=[vmem] * 4,
        scratch_shapes=[block(stages - 1 - s) for _ in range(2) for s in range(stages)]
        + [block(stages - 1 - s) for _ in range(2) for s in range(stages - 1)]
        + [block(stages)] * 2
        + [
            pltpu.VMEM((MOST_WIN,) + slots[2:], bf16),
            pltpu.VMEM(slots, bf16),
            pltpu.VMEM(slots, bf16),
            pltpu.VMEM((2, caplen, inner), bf16),
            pltpu.VMEM(w_query.shape, bf16),
            pltpu.VMEM(w_output.shape, bf16),
            dma((2 * stages,)),
            dma((2 * stages,)),
            dma((n_dev,)),
            dma((n_dev,)),
            dma((2,)),
            dma((2,)),
        ],
        compiler_params=pltpu.CompilerParams(
            collective_id=0, has_side_effects=True, vmem_limit_bytes=48 * 1024 * 1024
        ),
        name="tail",
    )(
        return_index, target, half, d_kv, memory_kv, part, x, grad_out,
        gain.reshape(1, model), w_query, w_output,
    )


def swap(x):
    return lax.ppermute(x, "section", [(0, 1), (1, 0)])


def local(
    frames,
    window_counts,
    learned_queries,
    frame_kv,
    query_out,
    query_gain,
    captions,
    caption_lengths,
    caption_gain,
    w_query,
    memory_kv,
    w_output,
    upstream,
):
    videos = lax.axis_size("dev")
    windows, _, width = frames.shape
    tokens = learned_queries.shape[0]
    inner = w_query.shape[1]
    caplen = captions.shape[2]
    per_slot = (MOST_WIN + videos - 2) // (videos - 1)
    section_id = lax.axis_index("section")
    video_id = lax.axis_index("dev")
    counts_row = lax.dynamic_index_in_dim(window_counts, section_id, 0, keepdims=False)
    run_ends = jnp.cumsum(counts_row)
    starts = run_ends - counts_row
    local_index = jnp.arange(windows, dtype=jnp.int32)
    ranked = (
        local_index // per_slot * (per_slot * videos) + video_id * per_slot + local_index % per_slot
    )
    owner_video = jnp.sum((run_ends[None, :] <= ranked[:, None]).astype(jnp.int32), axis=1)
    target = owner_video * per_slot + local_index % per_slot
    slot_index = jnp.arange(videos * per_slot, dtype=jnp.int32)
    send_index = jnp.sum(
        jnp.where(slot_index[:, None] == target[None, :], local_index[None, :], 0), axis=1
    )
    count_here = lax.dynamic_index_in_dim(counts_row, video_id, 0, keepdims=False)
    start_here = lax.dynamic_index_in_dim(starts, video_id, 0, keepdims=False)
    position = jnp.arange(MOST_WIN, dtype=jnp.int32)
    incoming = start_here + position
    source_slot = incoming // per_slot % videos * per_slot + incoming % per_slot
    present = position < count_here
    return_index = jnp.sum(
        jnp.where(
            (slot_index[:, None] == source_slot[None, :]) & present[None, :], position[None, :], 0
        ),
        axis=1,
    )
    live = (count_here * tokens).reshape(1)

    x = captions[0, 0].astype(jnp.float32)
    inv_rms = lax.rsqrt(jnp.mean(x * x, axis=-1, keepdims=True) + EPSILON)
    normed = (x * inv_rms * caption_gain).astype(jnp.bfloat16)
    row_live = jnp.arange(caplen, dtype=jnp.int32) < caption_lengths[0, 0]
    grad_out = jnp.where(row_live[:, None], upstream[0, 0], jnp.zeros_like(upstream[0, 0]))
    both, memory_half, key_value = head(
        send_index,
        source_slot,
        frames,
        learned_queries,
        frame_kv,
        query_out,
        query_gain,
        normed,
        grad_out,
        w_query,
        w_output,
        memory_kv,
    )

    stats = attention_stats(live, both[0], both[1], key_value)
    peer = swap(stats)
    peer = jnp.concatenate([peer[..., caplen:], peer[..., :caplen]], axis=-1)
    partial, d_kv = attention_grads(live, both[0], both[1], key_value, stats, peer)

    kv_grad, memory_grad, decoded, caption_grad = tail(
        return_index,
        target,
        memory_half,
        d_kv,
        memory_kv,
        partial,
        captions[0, 0],
        grad_out,
        caption_gain,
        w_query,
        w_output,
    )
    return decoded[None, None], caption_grad[None, None], memory_grad, kv_grad


def solution(mesh):
    return jax.shard_map(
        local,
        mesh=mesh,
        in_specs=(
            P(("section", "dev"), None, None),
            P(),
            P(),
            P(),
            P(),
            P(),
            P("section", "dev", None, None),
            P("section", "dev"),
            P(),
            P(),
            P(),
            P(),
            P("section", "dev", None, None),
        ),
        out_specs=(
            P("section", "dev", None, None),
            P("section", "dev", None, None),
            P(("section", "dev"), None, None),
            P(("section", "dev"), None),
        ),
        check_vma=False,
    )
```
